256 devices in a mesh: frame: 64 (over z, x, core), slab: 4 (over y).
Axes of the slice: x: 4, y: 4, z: 8, core: 2. Of those that a mesh axis runs over, the one named last changes fastest.
Arguments:
- latents: bfloat16 [128, 16, 160, 512], P('frame', 'slab'), may hold values from -20 to 20
- clip_starts: int32 [128], replicated, may hold values from 0 to 1
- w_space: bfloat16 [3, 3, 512, 512], replicated, may hold values from -0.09375 to 0.09375
- w_time: bfloat16 [3, 512, 512], replicated, may hold values from -0.15625 to 0.15625
- w_qkv: bfloat16 [512, 1536], replicated, may hold values from -0.25 to 0.25
- w_out: bfloat16 [512, 512], replicated, may hold values from -0.25 to 0.25
Outputs:
- block_out: bfloat16 [128, 16, 160, 512], P('frame', 'slab')
The draws below stay inside these ranges and needn't reach their ends.
All inputs are finite; a program needn't handle non-finite values.
Results may differ from the reference program's by a relative error of at most 0.0065.
Values may be sent and summed in bfloat16 or wider, within the bound.
No kernel may reach another device: no remote copies, remote signals or barrier semaphores. Data moves between devices by JAX's collectives and lax.ppermute only.
A program may use at most 64 MiB of HBM per device.

```python
import math
import jax
import jax.numpy as jnp
from jax import lax

C = 512
HEADS = 8
WIDTH = 160
FRAMES = 128
HEIGHT = 16


def draw_latents(key, part):
    key_one = jax.random.fold_in(jax.random.fold_in(key, 11), 0)
    values = jnp.clip(jax.random.normal(key_one, (FRAMES, HEIGHT, WIDTH, C), jnp.float32), -6.0, 6.0)
    return values.astype(jnp.bfloat16)


def draw_clip_starts(key, part):
    picked = jax.random.randint(jax.random.fold_in(key, 23), (FRAMES,), 0, 20)
    flagged = (picked == 0).astype(jnp.int32)
    return flagged.at[0].set(1)


def gaussian(own_key, dims, deviation, most, kind=jnp.bfloat16):
    return jnp.clip(deviation * jax.random.normal(own_key, dims, jnp.float32), -most, most).astype(kind)


def setup_inputs(seed: int = 0) -> dict:
    key_of = jax.random.split(jax.random.key(seed), 7)
    return {
        "latents": draw_latents(jax.random.fold_in(key_of[6], 71), 0),
        "clip_starts": draw_clip_starts(jax.random.fold_in(key_of[6], 71), 0),
        "w_space": gaussian(key_of[2], (3, 3, C, C), (9 * C) ** -0.5, 0.09375),
        "w_time": gaussian(key_of[3], (3, C, C), (3 * C) ** -0.5, 0.15625),
        "w_qkv": gaussian(key_of[4], (C, 3 * C), C ** -0.5, 0.25),
        "w_out": gaussian(key_of[5], (C, C), C ** -0.5, 0.25),
    }


def space_conv(padded_rows, w_space):
    frames, rows_padded, columns, channels = padded_rows.shape
    row_count = rows_padded - 2
    widened = jnp.pad(padded_rows, ((0, 0), (0, 0), (1, 1), (0, 0)))
    summed = jnp.zeros((frames * row_count * columns, channels), jnp.float32)
    for row_shift in range(3):
        for col_shift in range(3):
            source = widened[:, row_shift:row_shift + row_count, col_shift:col_shift + columns].reshape(-1, channels)
            summed = summed + jnp.dot(source, w_space[row_shift, col_shift], preferred_element_type=jnp.float32)
    return jax.nn.silu(summed).astype(jnp.bfloat16).reshape(frames, row_count, columns, channels)

def clip_window(clip_starts, first_frame, count):
    clip_ids = jnp.cumsum(clip_starts).astype(jnp.int32)
    padded = jnp.concatenate([jnp.full((2,), -1, jnp.int32), clip_ids])
    return lax.dynamic_slice_in_dim(padded, first_frame, count + 2)

def time_conv(extended, window, w_time):
    count = extended.shape[0] - 2
    middle = extended.shape[1:-1]
    channels = extended.shape[-1]
    summed = jnp.zeros((count,) + middle + (channels,), jnp.float32)
    for offset in range(3):
        source = extended[2 - offset:2 - offset + count].reshape(-1, channels)
        product = jnp.dot(source, w_time[offset], preferred_element_type=jnp.float32).reshape((count,) + middle + (channels,))
        allowed = (window[2 - offset:2 - offset + count] == window[2:]).astype(jnp.float32)
        summed = summed + product * allowed.reshape((count,) + (1,) * (len(middle) + 1))
    return summed.astype(jnp.bfloat16)

def project(mixed_in, w_qkv):
    frames, pixels, channels = mixed_in.shape
    flattened = jnp.dot(mixed_in.reshape(-1, channels), w_qkv, preferred_element_type=jnp.float32)
    queries = flattened[:, :channels].astype(jnp.bfloat16).reshape(frames, pixels, channels)
    keys_out = flattened[:, channels:2 * channels].astype(jnp.bfloat16).reshape(frames, pixels, channels)
    values = flattened[:, 2 * channels:].astype(jnp.bfloat16).reshape(frames, pixels, channels)
    return (queries, keys_out, values)

def attend(queries, keys_in, values, allowed, head_count):
    frames, pixels, channels = queries.shape
    head_size = channels // head_count
    query_f = queries.reshape(frames, pixels, head_count, head_size).astype(jnp.float32)
    key_f = keys_in.reshape(frames, pixels, head_count, head_size).astype(jnp.float32)
    value_f = values.reshape(frames, pixels, head_count, head_size).astype(jnp.float32)
    scores = jnp.einsum('iphd,jphd->phij', query_f, key_f) * (1.0 / math.sqrt(head_size))
    scores = jnp.where(allowed, scores, -1e+30)
    weights = jax.nn.softmax(scores, axis=-1).astype(jnp.bfloat16)
    attended = jnp.einsum('phij,jphd->iphd', weights.astype(jnp.float32), value_f)
    return attended.reshape(frames, pixels, channels).astype(jnp.bfloat16)

def reference(latents, clip_starts, w_space, w_time, w_qkv, w_out):
    total_frames, height, columns, channels = latents.shape

    def one_frame(frame_data):
        return space_conv(jnp.pad(frame_data, ((1, 1), (0, 0), (0, 0)))[None], w_space)[0]
    hidden = lax.map(one_frame, latents)
    window = clip_window(clip_starts, 0, total_frames)
    extended = jnp.concatenate([jnp.zeros((2, height, columns, channels), hidden.dtype), hidden])
    mixed_in = time_conv(extended, window, w_time)
    clip_ids = window[2:]
    positions = jnp.arange(total_frames)
    allowed = (positions[None, :] <= positions[:, None]) & (clip_ids[None, :] == clip_ids[:, None])

    def per_row(row_data):
        queries, keys_out, values = project(row_data, w_qkv)
        attended = attend(queries, keys_out, values, allowed, HEADS)
        return jnp.dot(attended.reshape(-1, channels), w_out, preferred_element_type=jnp.float32).astype(jnp.bfloat16).reshape(total_frames, columns, channels)
    att_out = jnp.moveaxis(lax.map(per_row, jnp.moveaxis(mixed_in, 1, 0)), 0, 1)
    return (latents.astype(jnp.float32) + att_out.astype(jnp.float32)).astype(jnp.bfloat16)
```

```python
import functools

import jax
import jax.numpy as jnp
from jax import lax
from jax.experimental import pallas as pl
from jax.experimental.pallas import tpu as pltpu
from jax.sharding import Mesh
from jax.sharding import PartitionSpec as P

HEADS = 8
FRAME = ("frame_0", "frame_1", "frame_2")
BF = jnp.bfloat16
F32 = jnp.float32
COLS = 160
CH = 512
PAIR = 2 * COLS
TOTAL = 128
VMEM = pl.BlockSpec(memory_space=pltpu.VMEM)
ANY = pl.BlockSpec(memory_space=pl.ANY)
PARAMS = pltpu.CompilerParams(vmem_limit_bytes=60000 * 1024)


def dot(a, b):
    return jnp.dot(a, b, preferred_element_type=F32)


def dot_t(a, b):
    return lax.dot_general(a, b, (((1,), (1,)), ((), ())), preferred_element_type=F32)


def iotas(rows, cols):
    i = lax.broadcasted_iota(jnp.int32, (rows, cols), 0)
    j = lax.broadcasted_iota(jnp.int32, (rows, cols), 1)
    return i, j


def one_hot(hit):
    return jnp.where(hit, 1.0, 0.0).astype(BF)


def row_source(i):
    head = i < 256
    tail = i - 256
    g = jnp.where(head, i >> 4, tail >> 2)
    k = jnp.where(head, (i >> 1) & 7, 8 + ((tail >> 1) & 1))
    return (i & 1) * COLS + 10 * g + k


def pack_matrix():
    i, j = iotas(PAIR, PAIR)
    return one_hot(row_source(i) == j)


def unpack_matrix():
    i, j = iotas(PAIR, PAIR)
    return one_hot(row_source(j) == i)


def fold_source(i):
    return ((i >> 2) & 3) * 64 + (i >> 4) * 4 + (i & 3)


def fold_matrix():
    i, j = iotas(256, 256)
    return one_hot(fold_source(i) == j)


def unfold_matrix():
    i, j = iotas(256, 256)
    return one_hot(fold_source(j) == i)


def lanes(x, l):
    return x[:, l * 128 : (l + 1) * 128]


def pack_row(y, pack, fold, store):
    p = dot(pack, y).astype(BF)
    for l in range(4):
        store(16 * l, lanes(p[:256], l).reshape(16, 16, 128))
    tail = jnp.concatenate([lanes(p[256:], l) for l in range(4)], axis=0)
    store(64, dot(fold, tail).astype(BF).reshape(16, 16, 128))


def silu(v):
    return v / (1.0 + jnp.exp(-v))


def spread(x, store):
    wide = x.astype(F32)
    i, _ = iotas(COLS, CH)
    before = jnp.where(i == 0, 0.0, pltpu.roll(wide, 1, 0))
    after = jnp.where(i == COLS - 1, 0.0, pltpu.roll(wide, COLS - 1, 0))
    store(0, before.astype(BF))
    store(1, x)
    store(2, after.astype(BF))


def spread_into(ref, first, x):
    def store(b, v):
        ref[pl.ds(first, COLS), pl.ds(b * CH, CH)] = v

    spread(x, store)


def conv_inner_kernel(x_ref, w_ref, out_ref, edge_ref, xs, pay, sem):
    for r in range(4):
        for f in range(2):
            spread_into(xs, r * PAIR + f * COLS, x_ref[f, r])
    pack, fold = pack_matrix(), fold_matrix()

    def tap(r, a):
        return dot(xs[pl.ds((r + a - 1) * PAIR, PAIR), :], w_ref[a])

    for r in (1, 2):
        y = silu(tap(r, 0) + tap(r, 1) + tap(r, 2)).astype(BF)

        def store(first, tiles, r=r):
            pay[pl.ds((r - 1) * 16, 16), pl.ds(first, 16), :] = tiles

        pack_row(y, pack, fold, store)
    copy = pltpu.make_async_copy(pay, out_ref.at[pl.ds(16, 32)], sem)
    copy.start()
    edge_ref[0] = tap(0, 1) + tap(0, 2)
    edge_ref[1] = tap(3, 0) + tap(3, 1)
    copy.wait()


def conv_edge_kernel(low_ref, high_ref, edge_ref, w_ref, held_ref, out_ref, xs, pay, sem):
    del held_ref
    for f in range(2):
        spread_into(xs, f * COLS, low_ref[f, 0])
        spread_into(xs, PAIR + f * COLS, high_ref[f, 0])
    pack, fold = pack_matrix(), fold_matrix()
    for n, a in ((0, 0), (1, 2)):
        y = silu(edge_ref[n] + dot(xs[pl.ds(n * PAIR, PAIR), :], w_ref[a])).astype(BF)

        def store(first, tiles, n=n):
            pay[n, :, pl.ds(first, 16), :] = tiles

        pack_row(y, pack, fold, store)
    copies = [
        pltpu.make_async_copy(pay.at[n], out_ref.at[pl.ds(48 * n, 16)], sem.at[n]) for n in range(2)
    ]
    for copy in copies:
        copy.start()
    for copy in copies:
        copy.wait()


def conv(latents, low, high, w_space):
    taps = w_space.reshape(3, 3 * CH, CH)
    payload = jax.ShapeDtypeStruct((64, 80, 128), BF)
    started, edge = pl.pallas_call(
        conv_inner_kernel,
        out_shape=(payload, jax.ShapeDtypeStruct((2, PAIR, CH), F32)),
        in_specs=[VMEM, VMEM],
        out_specs=(ANY, VMEM),
        scratch_shapes=[
            pltpu.VMEM((4 * PAIR, 3 * CH), BF),
            pltpu.VMEM((32, 80, 128), BF),
            pltpu.SemaphoreType.DMA,
        ],
        compiler_params=PARAMS,
        cost_estimate=pl.CostEstimate(
            flops=2 * 10 * PAIR * 3 * CH * CH, bytes_accessed=10 << 20, transcendentals=0
        ),
        name="conv_inner",
    )(latents, taps)
    return pl.pallas_call(
        conv_edge_kernel,
        out_shape=payload,
        in_specs=[VMEM, VMEM, VMEM, VMEM, ANY],
        out_specs=ANY,
        scratch_shapes=[
            pltpu.VMEM((2 * PAIR, 3 * CH), BF),
            pltpu.VMEM((2, 16, 80, 128), BF),
            pltpu.SemaphoreType.DMA((2,)),
        ],
        input_output_aliases={4: 0},
        compiler_params=PARAMS,
        name="conv_edge",
    )(low, high, edge, taps, started)


def gather_a(i):
    return ((i >> 1) & 7) * 16 + (i >> 4) * 2 + (i & 1)


def gather_b(i):
    return ((i >> 1) & 7) * 16 + (i >> 5) * 4 + ((i >> 4) & 1) * 2 + (i & 1)


def middle_kernel(
    x_ref, shift_ref, bias_ref, wt_ref, wq_ref, wo_ref, out_ref, xs, mixed, qkv, att, res
):
    i, j = iotas(128, 128)
    take_a, take_b = one_hot(gather_a(i) == j), one_hot(gather_b(i) == j)
    give_a, give_b = one_hot(gather_a(j) == i), one_hot(gather_b(j) == i)
    for n in range(8):
        part = jnp.concatenate(
            [x_ref[pl.ds(8 * n, 8), pl.ds(16 * l, 16), :].reshape(128, 128) for l in range(4)],
            axis=1,
        )
        rows = dot(take_a, part).astype(BF)
        for k in range(8):
            xs[pl.ds(k * TOTAL + 16 * n, 16), pl.ds(0, CH)] = rows[16 * k : 16 * k + 16]
        rows = dot(take_b, x_ref[pl.ds(8 * n, 8), pl.ds(64, 16), :].reshape(128, 128)).astype(BF)
        for l in range(4):
            for k in range(2):
                at = (2 * l + k) * 16
                xs[pl.ds((8 + k) * TOTAL + 16 * n, 16), pl.ds(128 * l, 128)] = rows[at : at + 16]
    shift = shift_ref[...]
    for k in range(10):
        moved = dot(shift, xs[pl.ds(k * TOTAL, TOTAL), pl.ds(0, CH)]).astype(BF)
        xs[pl.ds(k * TOTAL, TOTAL), pl.ds(CH, CH)] = moved[:TOTAL]
        xs[pl.ds(k * TOTAL, TOTAL), pl.ds(2 * CH, CH)] = moved[TOTAL:]
    for c in range(2):
        part = pl.ds(640 * c, 640)
        mixed[part, :] = dot(xs[part, :], wt_ref[...]).astype(BF)
        for t in range(3):
            cut = pl.ds(t * CH, CH)
            qkv[part, cut] = dot(mixed[part, :], wq_ref[:, cut]).astype(BF)

    bias = bias_ref[...]
    bias = jnp.concatenate([bias, bias], axis=0)
    _, lane = iotas(TOTAL, 128)
    left = lane < 64
    scale_l = jnp.where(left, 0.125, 0.0).astype(BF)
    scale_r = jnp.where(left, 0.0, 0.125).astype(BF)
    ones = jnp.ones((TOTAL, 128), BF)

    def pixel(k, carry):
        rows = pl.ds(pl.multiple_of(k * TOTAL, TOTAL), TOTAL)
        for h in range(4):
            q = qkv[rows, pl.ds(128 * h, 128)]
            key = qkv[rows, pl.ds(CH + 128 * h, 128)]
            v = qkv[rows, pl.ds(2 * CH + 128 * h, 128)]
            both = jnp.concatenate([q * scale_l, q * scale_r], axis=0)
            s = dot_t(both, key) + bias
            p = jnp.exp(s - jnp.max(s, axis=-1, keepdims=True)).astype(BF)
            o = dot(p, jnp.concatenate([v, ones], axis=1))
            o = o[:, :128] / o[:, 128:]
            att[rows, pl.ds(128 * h, 128)] = jnp.where(left, o[:TOTAL], o[TOTAL:]).astype(BF)
        return carry

    lax.fori_loop(0, 10, pixel, 0)
    for c in range(2):
        part = pl.ds(640 * c, 640)
        res[part, :] = dot(att[part, :], wo_ref[...]).astype(BF)
    for n in range(8):
        rows = jnp.concatenate(
            [res[pl.ds(k * TOTAL + 16 * n, 16), :] for k in range(8)], axis=0
        )
        part = dot(give_a, rows).astype(BF)
        for l in range(4):
            out_ref[pl.ds(8 * n, 8), pl.ds(16 * l, 16), :] = lanes(part, l).reshape(8, 16, 128)
        rows = jnp.concatenate(
            [
                res[pl.ds((8 + k) * TOTAL + 16 * n, 16), pl.ds(128 * l, 128)]
                for l in range(4)
                for k in range(2)
            ],
            axis=0,
        )
        out_ref[pl.ds(8 * n, 8), pl.ds(64, 16), :] = dot(give_b, rows).astype(BF).reshape(8, 16, 128)


def middle(arrived, clip_starts, w_time, w_qkv, w_out):
    clip_ids = jnp.cumsum(clip_starts)
    same = clip_ids[None, :] == clip_ids[:, None]
    i, j = iotas(TOTAL, TOTAL)
    bias = jnp.where(same & (j <= i), 0.0, -1e30).astype(F32)
    shift = jnp.concatenate([one_hot(same & (j == i - 1)), one_hot(same & (j == i - 2))], axis=0)
    return pl.pallas_call(
        middle_kernel,
        out_shape=jax.ShapeDtypeStruct((64, 80, 128), BF),
        in_specs=[VMEM] * 6,
        out_specs=VMEM,
        scratch_shapes=[
            pltpu.VMEM((1280, 3 * CH), BF),
            pltpu.VMEM((1280, CH), BF),
            pltpu.VMEM((1280, 3 * CH), BF),
            pltpu.VMEM((1280, CH), BF),
            pltpu.VMEM((1280, CH), BF),
        ],
        compiler_params=PARAMS,
        name="middle",
    )(arrived, shift, bias, w_time.reshape(3 * CH, CH), w_qkv, w_out)


def finish_kernel(x_ref, latent_ref, out_ref):
    unpack, unfold = unpack_matrix(), unfold_matrix()
    head = jnp.concatenate(
        [x_ref[:, pl.ds(16 * l, 16), :].reshape(256, 128) for l in range(4)], axis=1
    )
    tail = dot(unfold, x_ref[:, pl.ds(64, 16), :].reshape(256, 128)).astype(BF)
    tail = jnp.concatenate([tail[64 * l : 64 * l + 64] for l in range(4)], axis=1)
    y = dot(unpack, jnp.concatenate([head, tail], axis=0))
    for f in range(2):
        part = y[f * COLS : (f + 1) * COLS]
        out_ref[f, 0] = (latent_ref[f, 0].astype(F32) + part).astype(BF)


def finish(returned, latents):
    block = pl.BlockSpec((2, 1, COLS, CH), lambda r: (0, r, 0, 0))
    return pl.pallas_call(
        finish_kernel,
        out_shape=jax.ShapeDtypeStruct(latents.shape, BF),
        grid=(4,),
        in_specs=[pl.BlockSpec((16, 80, 128), lambda r: (r, 0, 0)), block],
        out_specs=block,
        compiler_params=PARAMS,
        name="finish",
    )(returned, latents)


def on_device(latents, clip_starts, w_space, w_time, w_qkv, w_out):
    count = lax.axis_size("slab")
    forward = [(i, i + 1) for i in range(count - 1)]
    backward = [(target, source) for source, target in forward]
    low = lax.ppermute(latents[:, 3:], "slab", forward)
    high = lax.ppermute(latents[:, :1], "slab", backward)
    payload = conv(latents, low, high, w_space)
    arrived = lax.all_to_all(payload, FRAME, split_axis=0, concat_axis=0, tiled=True)
    result = middle(arrived, clip_starts, w_time, w_qkv, w_out)
    returned = lax.all_to_all(result, FRAME, split_axis=0, concat_axis=0, tiled=True)
    return finish(returned, latents)


def solution(mesh):
    finer = Mesh(
        mesh.devices.reshape(8, 4, 2, mesh.shape["slab"]), ("frame_0", "frame_1", "frame_2", "slab")
    )
    return jax.shard_map(
        on_device,
        mesh=finer,
        in_specs=(P(FRAME, "slab", None, None), P(), P(), P(), P(), P()),
        out_specs=P(FRAME, "slab", None, None),
        check_vma=False,
    )
```

```python
import functools

import jax
import jax.numpy as jnp
from jax import lax
from jax.experimental import pallas as pl
from jax.experimental.pallas import tpu as pltpu
from jax.sharding import Mesh
from jax.sharding import PartitionSpec as P

HEADS = 8
FRAME = ("frame_0", "frame_1", "frame_2")
BF = jnp.bfloat16
F32 = jnp.float32
COLS = 160
CH = 512
PAIR = 2 * COLS
TOTAL = 128
VMEM = pl.BlockSpec(memory_space=pltpu.VMEM)
ANY = pl.BlockSpec(memory_space=pl.ANY)
HBM = pl.BlockSpec(memory_space=pltpu.HBM)


def far(x):
    return pltpu.with_memory_space_constraint(x, pltpu.HBM)
PARAMS = pltpu.CompilerParams(vmem_limit_bytes=20 * 1024 * 1024)


def dot(a, b):
    return jnp.dot(a, b, preferred_element_type=F32)


def dot_t(a, b):
    return lax.dot_general(a, b, (((1,), (1,)), ((), ())), preferred_element_type=F32)


def iotas(rows, cols):
    i = lax.broadcasted_iota(jnp.int32, (rows, cols), 0)
    j = lax.broadcasted_iota(jnp.int32, (rows, cols), 1)
    return i, j


def one_hot(hit):
    return jnp.where(hit, 1.0, 0.0).astype(BF)


def row_source(i):
    head = i < 256
    tail = i - 256
    g = jnp.where(head, i >> 4, tail >> 2)
    k = jnp.where(head, (i >> 1) & 7, 8 + ((tail >> 1) & 1))
    return (i & 1) * COLS + 10 * g + k


def pack_matrix():
    i, j = iotas(PAIR, PAIR)
    return one_hot(row_source(i) == j)


def unpack_matrix():
    i, j = iotas(PAIR, PAIR)
    return one_hot(row_source(j) == i)


def fold_source(i):
    return ((i >> 2) & 3) * 64 + (i >> 4) * 4 + (i & 3)


def fold_matrix():
    i, j = iotas(256, 256)
    return one_hot(fold_source(i) == j)


def unfold_matrix():
    i, j = iotas(256, 256)
    return one_hot(fold_source(j) == i)


def lanes(x, l):
    return x[:, l * 128 : (l + 1) * 128]


def pack_row(y, pack, fold, store):
    p = dot(pack, y).astype(BF)
    for l in range(4):
        store(16 * l, lanes(p[:256], l).reshape(16, 16, 128))
    tail = jnp.concatenate([lanes(p[256:], l) for l in range(4)], axis=0)
    store(64, dot(fold, tail).astype(BF).reshape(16, 16, 128))


def silu(v):
    return v / (1.0 + jnp.exp(-v))


def spread(x, store):
    wide = x.astype(F32)
    i, _ = iotas(COLS, CH)
    before = jnp.where(i == 0, 0.0, pltpu.roll(wide, 1, 0))
    after = jnp.where(i == COLS - 1, 0.0, pltpu.roll(wide, COLS - 1, 0))
    store(0, before.astype(BF))
    store(1, x)
    store(2, after.astype(BF))


def spread_into(ref, first, x):
    def store(b, v):
        ref[pl.ds(first, COLS), pl.ds(b * CH, CH)] = v

    spread(x, store)


def conv_inner_kernel(x_ref, w_any, out_ref, edge_ref, outer_ref, xs, pay, mid_tap, sem, sems):
    taps = (outer_ref.at[0], mid_tap, outer_ref.at[1])
    order = (1, 2, 0)
    weights = fetch([w_any.at[a] for a in order], [taps[a] for a in order], sems)
    for r in range(4):
        for f in range(2):
            spread_into(xs, r * PAIR + f * COLS, x_ref[f, r])
    pack, fold = pack_matrix(), fold_matrix()

    def tap(r, a):
        return dot(xs[pl.ds((r + a - 1) * PAIR, PAIR), :], taps[a][...])

    weights[0].wait()
    weights[1].wait()
    edge_ref[0] = tap(0, 1) + tap(0, 2)
    weights[2].wait()

    for r in (1, 2):
        y = silu(tap(r, 0) + tap(r, 1) + tap(r, 2)).astype(BF)

        def store(first, tiles, r=r):
            pay[pl.ds((r - 1) * 16, 16), pl.ds(first, 16), :] = tiles

        pack_row(y, pack, fold, store)
    copy = pltpu.make_async_copy(pay, out_ref.at[pl.ds(16, 32)], sem)
    copy.start()
    edge_ref[1] = tap(3, 0) + tap(3, 1)
    copy.wait()


def conv_edge_kernel(low_ref, high_ref, edge_ref, w_ref, held_ref, out_ref, xs, pay, sem):
    del held_ref
    for f in range(2):
        spread_into(xs, f * COLS, low_ref[f, 0])
        spread_into(xs, PAIR + f * COLS, high_ref[f, 0])
    pack, fold = pack_matrix(), fold_matrix()
    for n in range(2):
        y = silu(edge_ref[n] + dot(xs[pl.ds(n * PAIR, PAIR), :], w_ref[n])).astype(BF)

        def store(first, tiles, n=n):
            pay[n, :, pl.ds(first, 16), :] = tiles

        pack_row(y, pack, fold, store)
    copies = [
        pltpu.make_async_copy(pay.at[n], out_ref.at[pl.ds(48 * n, 16)], sem.at[n]) for n in range(2)
    ]
    for copy in copies:
        copy.start()
    for copy in copies:
        copy.wait()


def conv(latents, low, high, w_space):
    taps = far(w_space.reshape(3, 3 * CH, CH))
    payload = jax.ShapeDtypeStruct((64, 80, 128), BF)
    started, edge, outer = pl.pallas_call(
        conv_inner_kernel,
        out_shape=(
            payload,
            jax.ShapeDtypeStruct((2, PAIR, CH), F32),
            jax.ShapeDtypeStruct((2, 3 * CH, CH), BF),
        ),
        in_specs=[VMEM, HBM],
        out_specs=(ANY, VMEM, VMEM),
        scratch_shapes=[
            pltpu.VMEM((4 * PAIR, 3 * CH), BF),
            pltpu.VMEM((32, 80, 128), BF),
            pltpu.VMEM((3 * CH, CH), BF),
            pltpu.SemaphoreType.DMA,
            pltpu.SemaphoreType.DMA((3,)),
        ],
        compiler_params=PARAMS,
        cost_estimate=pl.CostEstimate(
            flops=2 * 10 * PAIR * 3 * CH * CH, bytes_accessed=10 << 20, transcendentals=0
        ),
        name="conv_inner",
    )(latents, taps)
    return pl.pallas_call(
        conv_edge_kernel,
        out_shape=payload,
        in_specs=[VMEM, VMEM, VMEM, VMEM, ANY],
        out_specs=ANY,
        scratch_shapes=[
            pltpu.VMEM((2 * PAIR, 3 * CH), BF),
            pltpu.VMEM((2, 16, 80, 128), BF),
            pltpu.SemaphoreType.DMA((2,)),
        ],
        input_output_aliases={4: 0},
        compiler_params=PARAMS,
        name="conv_edge",
    )(low, high, edge, outer, started)


def gather_a(i):
    return ((i >> 1) & 7) * 16 + (i >> 4) * 2 + (i & 1)


def gather_b(i):
    return ((i >> 1) & 7) * 16 + (i >> 5) * 4 + ((i >> 4) & 1) * 2 + (i & 1)


def fetch(sources, buffers, sems):
    copies = [
        pltpu.make_async_copy(source, buffer, sems.at[n])
        for n, (source, buffer) in enumerate(zip(sources, buffers))
    ]
    for copy in copies:
        copy.start()
    return copies


def middle_kernel(
    x_ref, shift_ref, bias_ref, wt_any, wq_any, wo_any, out_ref,
    xs, mixed, qkv, att, res, wt_ref, wq_ref, wo_ref, sems,
):
    weights = fetch((wt_any, wq_any, wo_any), (wt_ref, wq_ref, wo_ref), sems)
    i, j = iotas(128, 128)
    take_a, take_b = one_hot(gather_a(i) == j), one_hot(gather_b(i) == j)
    give_a, give_b = one_hot(gather_a(j) == i), one_hot(gather_b(j) == i)
    for n in range(8):
        part = jnp.concatenate(
            [x_ref[pl.ds(8 * n, 8), pl.ds(16 * l, 16), :].reshape(128, 128) for l in range(4)],
            axis=1,
        )
        rows = dot(take_a, part).astype(BF)
        for k in range(8):
            xs[pl.ds(k * TOTAL + 16 * n, 16), pl.ds(0, CH)] = rows[16 * k : 16 * k + 16]
        rows = dot(take_b, x_ref[pl.ds(8 * n, 8), pl.ds(64, 16), :].reshape(128, 128)).astype(BF)
        for l in range(4):
            for k in range(2):
                at = (2 * l + k) * 16
                xs[pl.ds((8 + k) * TOTAL + 16 * n, 16), pl.ds(128 * l, 128)] = rows[at : at + 16]
    shift = shift_ref[...]
    for k in range(10):
        moved = dot(shift, xs[pl.ds(k * TOTAL, TOTAL), pl.ds(0, CH)]).astype(BF)
        xs[pl.ds(k * TOTAL, TOTAL), pl.ds(CH, CH)] = moved[:TOTAL]
        xs[pl.ds(k * TOTAL, TOTAL), pl.ds(2 * CH, CH)] = moved[TOTAL:]
    weights[0].wait()
    weights[1].wait()
    for c in range(2):
        part = pl.ds(640 * c, 640)
        mixed[part, :] = dot(xs[part, :], wt_ref[...]).astype(BF)
        for t in range(3):
            cut = pl.ds(t * CH, CH)
            qkv[part, cut] = dot(mixed[part, :], wq_ref[:, cut]).astype(BF)

    bias = bias_ref[...]
    _, lane = iotas(TOTAL, 128)
    left = jnp.where(lane < 64, 1.0, 0.0).astype(BF)
    right = jnp.where(lane < 64, 0.0, 1.0).astype(BF)
    scale = BF(0.125)
    weigh = jnp.concatenate([left, right], axis=0)

    def pixel(k, carry):
        rows = pl.ds(pl.multiple_of(k * TOTAL, TOTAL), TOTAL)
        for h in range(4):
            q = qkv[rows, pl.ds(128 * h, 128)]
            key = qkv[rows, pl.ds(CH + 128 * h, 128)]
            v = qkv[rows, pl.ds(2 * CH + 128 * h, 128)]
            keys = jnp.concatenate([key * (left * scale), key * (right * scale)], axis=0)
            s = dot_t(q, keys)
            p = []
            for t in range(2):
                part = lanes(s, t) + bias
                p.append(jnp.exp(part - jnp.max(part, axis=-1, keepdims=True)).astype(BF))
            values = jnp.concatenate([jnp.concatenate([v * left, v * right], axis=0), weigh], axis=1)
            o = dot(jnp.concatenate(p, axis=1), values)
            att[rows, pl.ds(128 * h, 128)] = (o[:, :128] / o[:, 128:]).astype(BF)
        return carry

    lax.fori_loop(0, 10, pixel, 0, unroll=10)
    weights[2].wait()
    for c in range(2):
        part = pl.ds(640 * c, 640)
        res[part, :] = dot(att[part, :], wo_ref[...]).astype(BF)
    for n in range(8):
        rows = jnp.concatenate(
            [res[pl.ds(k * TOTAL + 16 * n, 16), :] for k in range(8)], axis=0
        )
        part = dot(give_a, rows).astype(BF)
        for l in range(4):
            out_ref[pl.ds(8 * n, 8), pl.ds(16 * l, 16), :] = lanes(part, l).reshape(8, 16, 128)
        rows = jnp.concatenate(
            [
                res[pl.ds((8 + k) * TOTAL + 16 * n, 16), pl.ds(128 * l, 128)]
                for l in range(4)
                for k in range(2)
            ],
            axis=0,
        )
        out_ref[pl.ds(8 * n, 8), pl.ds(64, 16), :] = dot(give_b, rows).astype(BF).reshape(8, 16, 128)


def middle(arrived, clip_starts, w_time, w_qkv, w_out):
    clip_ids = jnp.cumsum(clip_starts)
    same = clip_ids[None, :] == clip_ids[:, None]
    i, j = iotas(TOTAL, TOTAL)
    bias = jnp.where(same & (j <= i), 0.0, -1e30).astype(F32)
    shift = jnp.concatenate([one_hot(same & (j == i - 1)), one_hot(same & (j == i - 2))], axis=0)
    return pl.pallas_call(
        middle_kernel,
        out_shape=jax.ShapeDtypeStruct((64, 80, 128), BF),
        in_specs=[VMEM] * 3 + [HBM] * 3,
        out_specs=VMEM,
        scratch_shapes=[
            pltpu.VMEM((1280, 3 * CH), BF),
            pltpu.VMEM((1280, CH), BF),
            pltpu.VMEM((1280, 3 * CH), BF),
            pltpu.VMEM((1280, CH), BF),
            pltpu.VMEM((1280, CH), BF),
            pltpu.VMEM((3 * CH, CH), BF),
            pltpu.VMEM((CH, 3 * CH), BF),
            pltpu.VMEM((CH, CH), BF),
            pltpu.SemaphoreType.DMA((3,)),
        ],
        compiler_params=PARAMS,
        name="middle",
    )(arrived, shift, bias, far(w_time.reshape(3 * CH, CH)), far(w_qkv), far(w_out))


def finish_kernel(x_ref, latent_ref, out_ref):
    unpack, unfold = unpack_matrix(), unfold_matrix()
    head = jnp.concatenate(
        [x_ref[:, pl.ds(16 * l, 16), :].reshape(256, 128) for l in range(4)], axis=1
    )
    tail = dot(unfold, x_ref[:, pl.ds(64, 16), :].reshape(256, 128)).astype(BF)
    tail = jnp.concatenate([tail[64 * l : 64 * l + 64] for l in range(4)], axis=1)
    y = dot(unpack, jnp.concatenate([head, tail], axis=0))
    for f in range(2):
        part = y[f * COLS : (f + 1) * COLS]
        out_ref[f, 0] = (latent_ref[f, 0].astype(F32) + part).astype(BF)


def finish(returned, latents):
    block = pl.BlockSpec((2, 1, COLS, CH), lambda r: (0, r, 0, 0))
    return pl.pallas_call(
        finish_kernel,
        out_shape=jax.ShapeDtypeStruct(latents.shape, BF),
        grid=(4,),
        in_specs=[pl.BlockSpec((16, 80, 128), lambda r: (r, 0, 0)), block],
        out_specs=block,
        compiler_params=PARAMS,
        name="finish",
    )(returned, latents)


def on_device(latents, clip_starts, w_space, w_time, w_qkv, w_out):
    count = lax.axis_size("slab")
    forward = [(i, i + 1) for i in range(count - 1)]
    backward = [(target, source) for source, target in forward]
    low = lax.ppermute(latents[:, 3:], "slab", forward)
    high = lax.ppermute(latents[:, :1], "slab", backward)
    payload = conv(latents, low, high, w_space)
    arrived = lax.all_to_all(payload, FRAME, split_axis=0, concat_axis=0, tiled=True)
    result = middle(arrived, clip_starts, w_time, w_qkv, w_out)
    returned = lax.all_to_all(result, FRAME, split_axis=0, concat_axis=0, tiled=True)
    return finish(returned, latents)


def solution(mesh):
    finer = Mesh(
        mesh.devices.reshape(8, 4, 2, mesh.shape["slab"]), ("frame_0", "frame_1", "frame_2", "slab")
    )
    return jax.shard_map(
        on_device,
        mesh=finer,
        in_specs=(P(FRAME, "slab", None, None), P(), P(), P(), P(), P()),
        out_specs=P(FRAME, "slab", None, None),
        check_vma=False,
    )
```

```python
import functools

import jax
import jax.numpy as jnp
from jax import lax
from jax.experimental import pallas as pl
from jax.experimental.pallas import tpu as pltpu
from jax.sharding import Mesh
from jax.sharding import PartitionSpec as P

HEADS = 8
FRAME = ("frame_0", "frame_1", "frame_2")
BF = jnp.bfloat16
F32 = jnp.float32
COLS = 160
CH = 512
PAIR = 2 * COLS
TOTAL = 128
VMEM = pl.BlockSpec(memory_space=pltpu.VMEM)
ANY = pl.BlockSpec(memory_space=pl.ANY)
HBM = pl.BlockSpec(memory_space=pltpu.HBM)


def far(x):
    return pltpu.with_memory_space_constraint(x, pltpu.HBM)
PARAMS = pltpu.CompilerParams(vmem_limit_bytes=20 * 1024 * 1024)


def dot(a, b):
    return jnp.dot(a, b, preferred_element_type=F32)


def dot_t(a, b):
    return lax.dot_general(a, b, (((1,), (1,)), ((), ())), preferred_element_type=F32)


def iotas(rows, cols):
    i = lax.broadcasted_iota(jnp.int32, (rows, cols), 0)
    j = lax.broadcasted_iota(jnp.int32, (rows, cols), 1)
    return i, j


def one_hot(hit):
    return jnp.where(hit, 1.0, 0.0).astype(BF)


GROUP = ("frame_2", "frame_0", "frame_1")


def over(i, n, most):
    return (i * (65536 // n + 1)) >> 16


def lanes(x, l):
    return x[:, l * 128 : (l + 1) * 128]


def stack_lanes(x):
    return jnp.concatenate([lanes(x, l) for l in range(4)], axis=0)


def silu(v):
    return v / (1.0 + jnp.exp(-v))


def fetch(sources, buffers, sems):
    copies = [
        pltpu.make_async_copy(source, buffer, sems.at[n])
        for n, (source, buffer) in enumerate(zip(sources, buffers))
    ]
    for copy in copies:
        copy.start()
    return copies


def spread_into(ref, first, x):
    wide = x.astype(F32)
    i, _ = iotas(COLS, CH)
    before = jnp.where(i == 0, 0.0, pltpu.roll(wide, 1, 0))
    after = jnp.where(i == COLS - 1, 0.0, pltpu.roll(wide, COLS - 1, 0))
    for b, v in enumerate((before.astype(BF), x, after.astype(BF))):
        ref[pl.ds(first, COLS), pl.ds(b * CH, CH)] = v


def conv_inner_kernel(x_ref, w_any, out_ref, xs, taps, sems):
    order = (1, 2, 0)
    weights = fetch([w_any.at[a] for a in order], [taps.at[a] for a in order], sems)
    for r in range(4):
        for f in range(2):
            spread_into(xs, r * PAIR + f * COLS, x_ref[f, r])
    i, j = iotas(PAIR, PAIR)
    pack = one_hot((i & 1) * COLS + (i >> 1) == j)
    g = over(i, 40, PAIR)
    l = over(i - 40 * g, 10, 40)
    fold = one_hot(l * 80 + g * 10 + (i - 40 * g - 10 * l) == j)
    for copy in weights:
        copy.wait()
    for r in (1, 2):
        v = sum(dot(xs[pl.ds((r + a - 1) * PAIR, PAIR), :], taps[a]) for a in range(3))
        y = dot(pack, silu(v).astype(BF)).astype(BF)
        for n in range(4):
            block = dot(fold, stack_lanes(y[80 * n : 80 * n + 80])).astype(BF)
            out_ref[pl.ds((r - 1) * 16 + 4 * n, 4)] = block.reshape(4, 80, 128)


def conv_outer_kernel(x_ref, low_ref, high_ref, w_any, keep_ref, send_ref, xs, taps, sems):
    order = (1, 0, 2)
    weights = fetch([w_any.at[a] for a in order], [taps.at[a] for a in order], sems)
    for f in range(2):
        spread_into(xs, f * COLS, low_ref[f, 0])
        for r in range(4):
            spread_into(xs, (r + 1) * PAIR + f * COLS, x_ref[f, r])
        spread_into(xs, 5 * PAIR + f * COLS, high_ref[f, 0])
    for copy in weights:
        copy.wait()
    rows = []
    for r in (0, 3):
        v = sum(dot(xs[pl.ds((r + a) * PAIR, PAIR), :], taps[a]) for a in range(3))
        rows.append(silu(v))
    first = lax.axis_index("frame_2") == 0
    keep_ref[...] = jnp.where(first, rows[0], rows[1]).astype(BF)
    send_ref[...] = jnp.where(first, rows[1], rows[0]).astype(BF)


def taps_scratch(rows):
    return [
        pltpu.VMEM((rows * PAIR, 3 * CH), BF),
        pltpu.VMEM((3, 3 * CH, CH), BF),
        pltpu.SemaphoreType.DMA((3,)),
    ]


def conv_inner(latents, taps):
    out = pl.pallas_call(
        conv_inner_kernel,
        out_shape=jax.ShapeDtypeStruct((32, 80, 128), BF),
        in_specs=[VMEM, HBM],
        out_specs=VMEM,
        scratch_shapes=taps_scratch(4),
        compiler_params=PARAMS,
        cost_estimate=cost(6),
        name="conv_inner",
    )(latents, taps)
    return out.reshape(64, 40, 128)


def conv_outer(latents, low, high, taps):
    rows = jax.ShapeDtypeStruct((PAIR, CH), BF)
    return pl.pallas_call(
        conv_outer_kernel,
        out_shape=(rows, rows),
        in_specs=[VMEM, VMEM, VMEM, HBM],
        out_specs=(VMEM, VMEM),
        scratch_shapes=taps_scratch(6),
        compiler_params=PARAMS,
        cost_estimate=cost(6),
        name="conv_outer",
    )(latents, low, high, taps)


def cost(us):
    return pl.CostEstimate(flops=us * 900_000_000, bytes_accessed=1 << 20, transcendentals=0)


def to_x_kernel(keep_ref, came_ref, *outs):
    i, j = iotas(640, 640)
    d = over(i, 160, 640)
    r = i - 160 * d
    z = over(r, 20, 160)
    r = r - 20 * z
    x = (lax.axis_index("frame_1") + d) & 3
    source = ((r >> 1) & 1) * PAIR + (r & 1) * COLS + 5 * (z * 4 + x) + (r >> 2)
    y = dot(one_hot(source == j), jnp.concatenate([keep_ref[...], came_ref[...]], axis=0)).astype(BF)
    for n, out in enumerate(outs):
        out[...] = y[160 * n : 160 * n + 160]


def to_z_kernel(a, b, c, e, *outs):
    i, j = iotas(640, 640)
    d = over(i, 80, 640)
    r = i - 80 * d
    z = (lax.axis_index("frame_0") + d) & 7
    source = ((r >> 2) & 3) * 160 + z * 20 + (r >> 4) * 4 + (r & 3)
    y = dot(one_hot(source == j), jnp.concatenate([a[...], b[...], c[...], e[...]], axis=0)).astype(BF)
    for n, out in enumerate(outs):
        out[...] = y[80 * n : 80 * n + 80]


def relay(kernel, name, count, rows, *blocks):
    return pl.pallas_call(
        kernel,
        out_shape=[jax.ShapeDtypeStruct((rows, CH), BF)] * count,
        in_specs=[VMEM] * len(blocks),
        out_specs=[VMEM] * count,
        compiler_params=PARAMS,
        cost_estimate=cost(2),
        name=name,
    )(*blocks)


def attention(xs, shift_ref, bias_ref, weights, wt_ref, wq_ref, wo_ref, qkv, att, res):
    shift = shift_ref[...]
    for k in range(5):
        moved = dot(shift, xs[pl.ds(k * TOTAL, TOTAL), pl.ds(0, CH)]).astype(BF)
        xs[pl.ds(k * TOTAL, TOTAL), pl.ds(CH, CH)] = moved[:TOTAL]
        xs[pl.ds(k * TOTAL, TOTAL), pl.ds(2 * CH, CH)] = moved[TOTAL:]
    weights[0].wait()
    weights[1].wait()
    mixed = dot(xs[...], wt_ref[...]).astype(BF)
    for t in range(3):
        cut = pl.ds(t * CH, CH)
        qkv[:, cut] = dot(mixed, wq_ref[:, cut]).astype(BF)
    bias = bias_ref[...]
    _, lane = iotas(TOTAL, 128)
    left = jnp.where(lane < 64, 1.0, 0.0).astype(BF)
    right = jnp.where(lane < 64, 0.0, 1.0).astype(BF)
    scale = BF(0.125)
    weigh = jnp.concatenate([left, right], axis=0)
    for k in range(5):
        rows = pl.ds(k * TOTAL, TOTAL)
        for h in range(4):
            q = qkv[rows, pl.ds(128 * h, 128)]
            key = qkv[rows, pl.ds(CH + 128 * h, 128)]
            v = qkv[rows, pl.ds(2 * CH + 128 * h, 128)]
            keys = jnp.concatenate([key * (left * scale), key * (right * scale)], axis=0)
            s = dot_t(q, keys)
            p = []
            for t in range(2):
                part = lanes(s, t) + bias
                p.append(jnp.exp(part - jnp.max(part, axis=-1, keepdims=True)).astype(BF))
            values = jnp.concatenate([jnp.concatenate([v * left, v * right], axis=0), weigh], axis=1)
            o = dot(jnp.concatenate(p, axis=1), values)
            att[rows, pl.ds(128 * h, 128)] = (o[:, :128] / o[:, 128:]).astype(BF)
    weights[2].wait()
    res[...] = dot(att[...], wo_ref[...]).astype(BF)


def inner_kernel(
    x_ref, shift_ref, bias_ref, wt_any, wq_any, wo_any, res, xs, qkv, att, wt, wq, wo, sems
):
    weights = fetch((wt_any, wq_any, wo_any), (wt, wq, wo), sems)
    i, j = iotas(PAIR, PAIR)
    l = over(i, 80, PAIR)
    r = i - 80 * l
    take = one_hot(((r >> 1) & 7) * 40 + l * 10 + (r >> 4) * 2 + (r & 1) == j)
    for n in range(8):
        rows = dot(take, x_ref[pl.ds(4 * n, 4)].reshape(PAIR, 128)).astype(BF)
        for l in range(4):
            for k in range(5):
                at = l * 80 + k * 16
                xs[pl.ds(k * TOTAL + 16 * n, 16), pl.ds(128 * l, 128)] = rows[at : at + 16]
    attention(xs, shift_ref, bias_ref, weights, wt, wq, wo, qkv, att, res)


def gather_a(i):
    return ((i >> 1) & 7) * 16 + (i >> 4) * 2 + (i & 1)


def gather_b(i):
    return ((i >> 1) & 7) * 16 + (i >> 5) * 4 + ((i >> 4) & 1) * 2 + (i & 1)


def outer_kernel(
    *refs,
):
    blocks, refs = refs[:8], refs[8:]
    held, shift_ref, bias_ref, wt_any, wq_any, wo_any, out_ref, *refs = refs
    xs, qkv, att, res, wt, wq, wo, sems = refs
    weights = fetch((wt_any, wq_any, wo_any), (wt, wq, wo), sems)
    i, j = iotas(TOTAL, TOTAL)
    z = (lax.axis_index("frame_0") + 8 - (j >> 4)) & 7
    x = (lax.axis_index("frame_1") + 4 - ((j >> 2) & 3)) & 3
    c = (lax.axis_index("frame_2") + ((j >> 1) & 1)) & 1
    place = one_hot(c * 64 + (z * 4 + x) * 2 + (j & 1) == i)
    for k in range(5):
        rows = jnp.concatenate([block[pl.ds(16 * k, 16), :] for block in blocks], axis=0)
        xs[pl.ds(k * TOTAL, TOTAL), pl.ds(0, CH)] = dot(place, rows).astype(BF)
    attention(xs, shift_ref, bias_ref, weights, wt, wq, wo, qkv, att, res)
    give_a, give_b = one_hot(gather_a(j) == i), one_hot(gather_b(j) == i)

    def piece(k, n):
        ref = held if k < 5 else res
        return ref[pl.ds((k % 5) * TOTAL + 16 * n, 16), :]

    for n in range(8):
        part = dot(give_a, jnp.concatenate([piece(k, n) for k in range(8)], axis=0)).astype(BF)
        for l in range(4):
            out_ref[pl.ds(8 * n, 8), pl.ds(16 * l, 16), :] = lanes(part, l).reshape(8, 16, 128)
        rows = jnp.concatenate([lanes(piece(8 + k, n), l) for l in range(4) for k in range(2)], axis=0)
        out_ref[pl.ds(8 * n, 8), pl.ds(64, 16), :] = dot(give_b, rows).astype(BF).reshape(8, 16, 128)


def core_scratch():
    return [
        pltpu.VMEM((3 * CH, CH), BF),
        pltpu.VMEM((CH, 3 * CH), BF),
        pltpu.VMEM((CH, CH), BF),
        pltpu.SemaphoreType.DMA((3,)),
    ]


def masks(clip_starts):
    i, j = iotas(TOTAL, TOTAL)

    def frame(n):
        return ((n >> 1) & 31) * 4 + (n >> 6) * 2 + (n & 1)

    clip_ids = jnp.cumsum(clip_starts)
    clip_ids = clip_ids.reshape(32, 2, 2).transpose(1, 0, 2).reshape(TOTAL)
    same = clip_ids[None, :] == clip_ids[:, None]
    i, j = frame(i), frame(j)
    bias = jnp.where(same & (j <= i), 0.0, -1e30).astype(F32)
    shift = jnp.concatenate([one_hot(same & (j == i - 1)), one_hot(same & (j == i - 2))], axis=0)
    return shift, bias


def inner(arrived, *rest):
    return pl.pallas_call(
        inner_kernel,
        out_shape=jax.ShapeDtypeStruct((640, CH), BF),
        in_specs=[VMEM] * 3 + [HBM] * 3,
        out_specs=VMEM,
        scratch_shapes=[
            pltpu.VMEM((640, 3 * CH), BF),
            pltpu.VMEM((640, 3 * CH), BF),
            pltpu.VMEM((640, CH), BF),
            *core_scratch(),
        ],
        compiler_params=PARAMS,
        cost_estimate=cost(7),
        name="inner",
    )(arrived.reshape(32, 80, 128), *rest)


def outer(blocks, held, *rest):
    return pl.pallas_call(
        outer_kernel,
        out_shape=jax.ShapeDtypeStruct((64, 80, 128), BF),
        in_specs=[VMEM] * 11 + [HBM] * 3,
        out_specs=VMEM,
        scratch_shapes=[
            pltpu.VMEM((640, 3 * CH), BF),
            pltpu.VMEM((640, 3 * CH), BF),
            pltpu.VMEM((640, CH), BF),
            pltpu.VMEM((640, CH), BF),
            *core_scratch(),
        ],
        compiler_params=PARAMS,
        cost_estimate=cost(8),
        name="outer",
    )(*blocks, held, *rest)


def finish_kernel(x_ref, latent_ref, out_ref):
    i, j = iotas(512, 512)
    unfold = one_hot(((i >> 2) & 31) * 16 + (i >> 7) * 4 + (i & 3) == j)
    i, j = iotas(640, 640)
    head = j < 512
    tail = j - 512
    g = jnp.where(head, j >> 4, tail >> 2)
    k = jnp.where(head, (j >> 1) & 7, 8 + ((tail >> 1) & 1))
    to = (j & 1) * COLS + 5 * g + jnp.where(k < 5, k, k + PAIR - 5)
    unpack = one_hot(to == i)
    for c in range(2):
        part = pl.ds(32 * c, 32)
        rows = jnp.concatenate(
            [x_ref[part, pl.ds(16 * l, 16), :].reshape(512, 128) for l in range(4)], axis=1
        )
        last = dot(unfold, x_ref[part, pl.ds(64, 16), :].reshape(512, 128)).astype(BF)
        last = jnp.concatenate([last[128 * l : 128 * l + 128] for l in range(4)], axis=1)
        y = dot(unpack, jnp.concatenate([rows, last], axis=0))
        for n, r in enumerate((1 + c, 3 * c)):
            for f in range(2):
                add = y[(2 * n + f) * COLS : (2 * n + f + 1) * COLS]
                out_ref[f, r] = (latent_ref[f, r].astype(F32) + add).astype(BF)


def finish(returned, latents):
    return pl.pallas_call(
        finish_kernel,
        out_shape=jax.ShapeDtypeStruct(latents.shape, BF),
        in_specs=[VMEM, VMEM],
        out_specs=VMEM,
        compiler_params=PARAMS,
        name="finish",
    )(returned, latents)


def turn(x, axis, step):
    count = lax.axis_size(axis)
    return lax.ppermute(x, axis, [(i, (i + step) % count) for i in range(count)])


def on_device(latents, clip_starts, w_space, w_time, w_qkv, w_out):
    count = lax.axis_size("slab")
    forward = [(i, i + 1) for i in range(count - 1)]
    backward = [(target, source) for source, target in forward]
    low = lax.ppermute(latents[:, 3:], "slab", forward)
    high = lax.ppermute(latents[:, :1], "slab", backward)
    taps = far(w_space.reshape(3, 3 * CH, CH))
    payload = conv_inner(latents, taps)
    arrived = lax.all_to_all(payload, GROUP, split_axis=0, concat_axis=0, tiled=True)
    keep, send = conv_outer(latents, low, high, taps)
    came = turn(send, "frame_2", 1)
    blocks = relay(to_x_kernel, "to_x", 4, 160, keep, came)
    blocks = [turn(b, "frame_1", n) if n else b for n, b in enumerate(blocks)]
    blocks = relay(to_z_kernel, "to_z", 8, 80, *blocks)
    blocks = [turn(b, "frame_0", n) if n else b for n, b in enumerate(blocks)]
    rest = (*masks(clip_starts), far(w_time.reshape(3 * CH, CH)), far(w_qkv), far(w_out))
    held = inner(arrived, *rest)
    result = outer(blocks, held, *rest)
    returned = lax.all_to_all(result, GROUP, split_axis=0, concat_axis=0, tiled=True)
    return finish(returned, latents)


def solution(mesh):
    finer = Mesh(
        mesh.devices.reshape(8, 4, 2, mesh.shape["slab"]), ("frame_0", "frame_1", "frame_2", "slab")
    )
    return jax.shard_map(
        on_device,
        mesh=finer,
        in_specs=(P(FRAME, "slab", None, None), P(), P(), P(), P(), P()),
        out_specs=P(FRAME, "slab", None, None),
        check_vma=False,
    )
```

```python
import functools

import jax
import jax.numpy as jnp
from jax import lax
from jax.experimental import pallas as pl
from jax.experimental.pallas import tpu as pltpu
from jax.sharding import Mesh
from jax.sharding import PartitionSpec as P

HEADS = 8
FRAME = ("frame_0", "frame_1", "frame_2")
BF = jnp.bfloat16
F32 = jnp.float32
COLS = 160
CH = 512
PAIR = 2 * COLS
TOTAL = 128
VMEM = pl.BlockSpec(memory_space=pltpu.VMEM)
ANY = pl.BlockSpec(memory_space=pl.ANY)
HBM = pl.BlockSpec(memory_space=pltpu.HBM)


def far(x):
    return pltpu.with_memory_space_constraint(x, pltpu.HBM)
PARAMS = pltpu.CompilerParams(vmem_limit_bytes=20 * 1024 * 1024)


def dot(a, b):
    return jnp.dot(a, b, preferred_element_type=F32)


def dot_t(a, b):
    return lax.dot_general(a, b, (((1,), (1,)), ((), ())), preferred_element_type=F32)


def iotas(rows, cols):
    i = lax.broadcasted_iota(jnp.int32, (rows, cols), 0)
    j = lax.broadcasted_iota(jnp.int32, (rows, cols), 1)
    return i, j


def one_hot(hit):
    return jnp.where(hit, 1.0, 0.0).astype(BF)


def tail_source(i):
    return ((i >> 2) & 3) * 64 + (i & 1) * 32 + 2 * (i >> 4) + ((i >> 1) & 1)


def lanes(x, l):
    return x[:, l * 128 : (l + 1) * 128]


def stack_lanes(x):
    return jnp.concatenate([lanes(x, l) for l in range(4)], axis=0)


def tail_matrix():
    i, j = iotas(256, 256)
    return one_hot(tail_source(i) == j)


def pack_row(y, tail, store):
    halves = [y[f * COLS : f * COLS + 128].reshape(16, 8, CH) for f in range(2)]
    head = jnp.concatenate(halves, axis=1).astype(BF)
    for l in range(4):
        store(16 * l, head[:, :, l * 128 : (l + 1) * 128])
    rest = jnp.concatenate([y[f * COLS + 128 : (f + 1) * COLS] for f in range(2)], axis=0)
    store(64, dot(tail, stack_lanes(rest.astype(BF))).astype(BF).reshape(16, 16, 128))


def silu(v):
    return v / (1.0 + jnp.exp(-v))


def spread(x, store):
    wide = x.astype(F32)
    i, _ = iotas(COLS, CH)
    before = jnp.where(i == 0, 0.0, pltpu.roll(wide, 1, 0))
    after = jnp.where(i == COLS - 1, 0.0, pltpu.roll(wide, COLS - 1, 0))
    store(0, x)
    store(1, before.astype(BF))
    store(2, after.astype(BF))


def spread_into(ref, first, x):
    def store(b, v):
        ref[pl.ds(first, COLS), pl.ds(b * CH, CH)] = v

    spread(x, store)


def conv_inner_kernel(
    x_ref, w_any, out_ref, edge_ref, outer_ref, xs, pay, pay_sum, mid_tap, sem, sems
):
    taps = (outer_ref.at[0], mid_tap, outer_ref.at[1])
    order = [(a, b) for a in (1, 2, 0) for b in (1, 0, 2)]
    spot = (1, 0, 2)
    weights = fetch(
        [w_any.at[a, pl.ds(b * CH, CH)] for a, b in order],
        [taps[a].at[pl.ds(spot[b] * CH, CH)] for a, b in order],
        sems,
    )
    weights[0].wait()
    centre = []
    for r in range(4):
        x = jnp.concatenate([x_ref[0, r], x_ref[1, r]], axis=0)
        centre.append(dot(x, mid_tap[pl.ds(0, CH), :]))
    edge_ref[0] = centre[0]
    edge_ref[1] = centre[3]
    for n in range(2):
        pay_sum[n] = centre[1 + n]
    for r in range(4):
        for f in range(2):
            spread_into(xs, r * PAIR + f * COLS, x_ref[f, r])
    tail = tail_matrix()

    def tap(r, a):
        return dot(xs[pl.ds((r + a - 1) * PAIR, PAIR), :], taps[a][...])

    def sides(r):
        return dot(xs[pl.ds(r * PAIR, PAIR), pl.ds(CH, 2 * CH)], mid_tap[pl.ds(CH, 2 * CH), :])

    for copy in weights[1:6]:
        copy.wait()
    edge_ref[0] = edge_ref[0] + sides(0) + tap(0, 2)
    for copy in weights[6:]:
        copy.wait()
    for r in (1, 2):
        y = silu(pay_sum[r - 1] + sides(r) + tap(r, 0) + tap(r, 2))

        def store(first, tiles, r=r):
            pay[pl.ds((r - 1) * 16, 16), pl.ds(first, 16), :] = tiles

        pack_row(y, tail, store)
    copy = pltpu.make_async_copy(pay, out_ref.at[pl.ds(16, 32)], sem)
    copy.start()
    edge_ref[1] = edge_ref[1] + sides(3) + tap(3, 0)
    copy.wait()


def conv_edge_kernel(low_ref, high_ref, edge_ref, w_ref, held_ref, out_ref, xs, pay, sem):
    del held_ref
    for f in range(2):
        spread_into(xs, f * COLS, low_ref[f, 0])
        spread_into(xs, PAIR + f * COLS, high_ref[f, 0])
    tail = tail_matrix()
    copies = []
    for n in range(2):
        y = silu(edge_ref[n] + dot(xs[pl.ds(n * PAIR, PAIR), :], w_ref[n]))

        def store(first, tiles, n=n):
            pay[n, :, pl.ds(first, 16), :] = tiles

        pack_row(y, tail, store)
        copies.append(
            pltpu.make_async_copy(pay.at[n], out_ref.at[pl.ds(48 * n, 16)], sem.at[n])
        )
        copies[n].start()
    for copy in copies:
        copy.wait()


def conv(latents, low, high, w_space):
    taps = far(w_space.reshape(3, 3 * CH, CH))
    payload = jax.ShapeDtypeStruct((64, 80, 128), BF)
    started, edge, outer = pl.pallas_call(
        conv_inner_kernel,
        out_shape=(
            payload,
            jax.ShapeDtypeStruct((2, PAIR, CH), F32),
            jax.ShapeDtypeStruct((2, 3 * CH, CH), BF),
        ),
        in_specs=[VMEM, HBM],
        out_specs=(ANY, VMEM, VMEM),
        scratch_shapes=[
            pltpu.VMEM((4 * PAIR, 3 * CH), BF),
            pltpu.VMEM((32, 80, 128), BF),
            pltpu.VMEM((2, PAIR, CH), F32),
            pltpu.VMEM((3 * CH, CH), BF),
            pltpu.SemaphoreType.DMA,
            pltpu.SemaphoreType.DMA((9,)),
        ],
        compiler_params=PARAMS,
        cost_estimate=pl.CostEstimate(
            flops=2 * 10 * PAIR * 3 * CH * CH, bytes_accessed=10 << 20, transcendentals=0
        ),
        name="conv_inner",
    )(latents, taps)
    return pl.pallas_call(
        conv_edge_kernel,
        out_shape=payload,
        in_specs=[VMEM, VMEM, VMEM, VMEM, ANY],
        out_specs=ANY,
        scratch_shapes=[
            pltpu.VMEM((2 * PAIR, 3 * CH), BF),
            pltpu.VMEM((2, 16, 80, 128), BF),
            pltpu.SemaphoreType.DMA((2,)),
        ],
        input_output_aliases={4: 0},
        compiler_params=PARAMS,
        name="conv_edge",
    )(low, high, edge, outer, started)


def gather_a(i):
    return ((i >> 1) & 7) * 16 + (i & 1) * 8 + (i >> 4)


def gather_b(i):
    return ((i >> 1) & 7) * 16 + (i >> 5) * 4 + ((i >> 4) & 1) * 2 + (i & 1)


def fetch(sources, buffers, sems):
    copies = [
        pltpu.make_async_copy(source, buffer, sems.at[n])
        for n, (source, buffer) in enumerate(zip(sources, buffers))
    ]
    for copy in copies:
        copy.start()
    return copies


def middle_kernel(
    x_ref, shift_ref, bias_ref, wt_any, wq_any, wo_any, out_ref,
    xs, mixed, qkv, att, res, wt_ref, wq_ref, wo_ref, sems,
):
    weights = fetch((wt_any, wq_any, wo_any), (wt_ref, wq_ref, wo_ref), sems)
    i, j = iotas(128, 128)
    take_a, take_b = one_hot(gather_a(i) == j), one_hot(gather_b(i) == j)
    give_a, give_b = one_hot(gather_a(j) == i), one_hot(gather_b(j) == i)
    for n in range(8):
        part = jnp.concatenate(
            [x_ref[pl.ds(8 * n, 8), pl.ds(16 * l, 16), :].reshape(128, 128) for l in range(4)],
            axis=1,
        )
        rows = dot(take_a, part).astype(BF)
        for k in range(8):
            xs[pl.ds(k * TOTAL + 16 * n, 16), pl.ds(0, CH)] = rows[16 * k : 16 * k + 16]
        rows = dot(take_b, x_ref[pl.ds(8 * n, 8), pl.ds(64, 16), :].reshape(128, 128)).astype(BF)
        for l in range(4):
            for k in range(2):
                at = (2 * l + k) * 16
                xs[pl.ds((8 + k) * TOTAL + 16 * n, 16), pl.ds(128 * l, 128)] = rows[at : at + 16]
    shift = shift_ref[...]
    for k in range(10):
        moved = dot(shift, xs[pl.ds(k * TOTAL, TOTAL), pl.ds(0, CH)]).astype(BF)
        xs[pl.ds(k * TOTAL, TOTAL), pl.ds(CH, CH)] = moved[:TOTAL]
        xs[pl.ds(k * TOTAL, TOTAL), pl.ds(2 * CH, CH)] = moved[TOTAL:]
    weights[0].wait()
    weights[1].wait()
    for c in range(2):
        part = pl.ds(640 * c, 640)
        mixed[part, :] = dot(xs[part, :], wt_ref[...]).astype(BF)
        for t in range(3):
            cut = pl.ds(t * CH, CH)
            qkv[part, cut] = dot(mixed[part, :], wq_ref[:, cut]).astype(BF)

    bias = bias_ref[...]
    _, lane = iotas(TOTAL, 128)
    left = jnp.where(lane < 64, 1.0, 0.0).astype(BF)
    right = jnp.where(lane < 64, 0.0, 1.0).astype(BF)
    scale = BF(0.125)
    weigh = jnp.concatenate([left, right], axis=0)

    def pixel(k, carry):
        rows = pl.ds(pl.multiple_of(k * TOTAL, TOTAL), TOTAL)
        for h in range(4):
            q = qkv[rows, pl.ds(128 * h, 128)]
            key = qkv[rows, pl.ds(CH + 128 * h, 128)]
            v = qkv[rows, pl.ds(2 * CH + 128 * h, 128)]
            keys = jnp.concatenate([key * (left * scale), key * (right * scale)], axis=0)
            s = dot_t(q, keys)
            p = []
            for t in range(2):
                part = lanes(s, t) + bias
                p.append(jnp.exp(part - jnp.max(part, axis=-1, keepdims=True)).astype(BF))
            values = jnp.concatenate([jnp.concatenate([v * left, v * right], axis=0), weigh], axis=1)
            o = dot(jnp.concatenate(p, axis=1), values)
            att[rows, pl.ds(128 * h, 128)] = (o[:, :128] / o[:, 128:]).astype(BF)
        return carry

    lax.fori_loop(0, 10, pixel, 0, unroll=10)
    weights[2].wait()
    for c in range(2):
        part = pl.ds(640 * c, 640)
        res[part, :] = dot(att[part, :], wo_ref[...]).astype(BF)
    for n in range(8):
        rows = jnp.concatenate(
            [res[pl.ds(k * TOTAL + 16 * n, 16), :] for k in range(8)], axis=0
        )
        part = dot(give_a, rows).astype(BF)
        for l in range(4):
            out_ref[pl.ds(8 * n, 8), pl.ds(16 * l, 16), :] = lanes(part, l).reshape(8, 16, 128)
        rows = jnp.concatenate(
            [
                res[pl.ds((8 + k) * TOTAL + 16 * n, 16), pl.ds(128 * l, 128)]
                for l in range(4)
                for k in range(2)
            ],
            axis=0,
        )
        out_ref[pl.ds(8 * n, 8), pl.ds(64, 16), :] = dot(give_b, rows).astype(BF).reshape(8, 16, 128)


def middle(arrived, clip_starts, w_time, w_qkv, w_out):
    clip_ids = jnp.cumsum(clip_starts)
    same = clip_ids[None, :] == clip_ids[:, None]
    i, j = iotas(TOTAL, TOTAL)
    bias = jnp.where(same & (j <= i), 0.0, -1e30).astype(F32)
    shift = jnp.concatenate([one_hot(same & (j == i - 1)), one_hot(same & (j == i - 2))], axis=0)
    return pl.pallas_call(
        middle_kernel,
        out_shape=jax.ShapeDtypeStruct((64, 80, 128), BF),
        in_specs=[VMEM] * 3 + [HBM] * 3,
        out_specs=VMEM,
        scratch_shapes=[
            pltpu.VMEM((1280, 3 * CH), BF),
            pltpu.VMEM((1280, CH), BF),
            pltpu.VMEM((1280, 3 * CH), BF),
            pltpu.VMEM((1280, CH), BF),
            pltpu.VMEM((1280, CH), BF),
            pltpu.VMEM((3 * CH, CH), BF),
            pltpu.VMEM((CH, 3 * CH), BF),
            pltpu.VMEM((CH, CH), BF),
            pltpu.SemaphoreType.DMA((3,)),
        ],
        compiler_params=PARAMS,
        name="middle",
    )(arrived, shift, bias, far(w_time.reshape(3 * CH, CH)), far(w_qkv), far(w_out))


def finish_kernel(x_ref, latent_ref, out_any, out, sems):
    i, j = iotas(256, 256)
    spread_tail = one_hot(tail_source(j) == i)
    copies = []
    for r in range(4):
        part = pl.ds(16 * r, 16)
        head = [x_ref[part, pl.ds(16 * l, 16), :].astype(F32) for l in range(4)]
        rest = dot(spread_tail, x_ref[part, pl.ds(64, 16), :].reshape(256, 128))
        for f in range(2):
            for l in range(4):
                cut = pl.ds(128 * l, 128)
                add = head[l][:, 8 * f : 8 * f + 8].reshape(128, 128)
                old = latent_ref[f, r, pl.ds(0, 128), cut].astype(F32)
                out[r, f, pl.ds(0, 128), cut] = (old + add).astype(BF)
                at = 64 * l + 32 * f
                old = latent_ref[f, r, pl.ds(128, 32), cut].astype(F32)
                out[r, f, pl.ds(128, 32), cut] = (old + rest[at : at + 32]).astype(BF)
        copies.append(pltpu.make_async_copy(out.at[r], out_any.at[:, r], sems.at[r]))
        copies[r].start()
    for copy in copies:
        copy.wait()


def finish(returned, latents):
    return pl.pallas_call(
        finish_kernel,
        out_shape=jax.ShapeDtypeStruct(latents.shape, BF),
        in_specs=[VMEM, VMEM],
        out_specs=ANY,
        scratch_shapes=[pltpu.VMEM((4, 2, COLS, CH), BF), pltpu.SemaphoreType.DMA((4,))],
        compiler_params=PARAMS,
        name="finish",
    )(returned, latents)


def on_device(latents, clip_starts, w_space, w_time, w_qkv, w_out):
    count = lax.axis_size("slab")
    forward = [(i, i + 1) for i in range(count - 1)]
    backward = [(target, source) for source, target in forward]
    low = lax.ppermute(latents[:, 3:], "slab", forward)
    high = lax.ppermute(latents[:, :1], "slab", backward)
    payload = conv(latents, low, high, w_space)
    arrived = lax.all_to_all(payload, FRAME, split_axis=0, concat_axis=0, tiled=True)
    result = middle(arrived, clip_starts, w_time, w_qkv, w_out)
    returned = lax.all_to_all(result, FRAME, split_axis=0, concat_axis=0, tiled=True)
    return finish(returned, latents)


def solution(mesh):
    finer = Mesh(
        mesh.devices.reshape(8, 4, 2, mesh.shape["slab"]), ("frame_0", "frame_1", "frame_2", "slab")
    )
    return jax.shard_map(
        on_device,
        mesh=finer,
        in_specs=(P(FRAME, "slab", None, None), P(), P(), P(), P(), P()),
        out_specs=P(FRAME, "slab", None, None),
        check_vma=False,
    )
```

```python
import functools

import jax
import jax.numpy as jnp
from jax import lax
from jax.experimental import pallas as pl
from jax.experimental.pallas import tpu as pltpu
from jax.sharding import Mesh
from jax.sharding import PartitionSpec as P

HEADS = 8
FRAME = ("frame_0", "frame_1", "frame_2")
BF = jnp.bfloat16
F32 = jnp.float32
COLS = 160
CH = 512
PAIR = 2 * COLS
TOTAL = 128
VMEM = pl.BlockSpec(memory_space=pltpu.VMEM)
ANY = pl.BlockSpec(memory_space=pl.ANY)
HBM = pl.BlockSpec(memory_space=pltpu.HBM)


def far(x):
    return pltpu.with_memory_space_constraint(x, pltpu.HBM)
PARAMS = pltpu.CompilerParams(vmem_limit_bytes=20 * 1024 * 1024)


def dot(a, b):
    return jnp.dot(a, b, preferred_element_type=F32)


def dot_t(a, b):
    return lax.dot_general(a, b, (((1,), (1,)), ((), ())), preferred_element_type=F32)


def iotas(rows, cols):
    i = lax.broadcasted_iota(jnp.int32, (rows, cols), 0)
    j = lax.broadcasted_iota(jnp.int32, (rows, cols), 1)
    return i, j


def one_hot(hit):
    return jnp.where(hit, 1.0, 0.0).astype(BF)


def tail_source(i):
    return ((i >> 2) & 3) * 64 + (i & 1) * 32 + 2 * (i >> 4) + ((i >> 1) & 1)


def lanes(x, l):
    return x[:, l * 128 : (l + 1) * 128]


def stack_lanes(x):
    return jnp.concatenate([lanes(x, l) for l in range(4)], axis=0)


def tail_matrix():
    i, j = iotas(256, 256)
    return one_hot(tail_source(i) == j)


def pack_row(y, tail, store):
    halves = [y[f * COLS : f * COLS + 128].reshape(16, 8, CH) for f in range(2)]
    head = jnp.concatenate(halves, axis=1).astype(BF)
    for l in range(4):
        store(16 * l, head[:, :, l * 128 : (l + 1) * 128])
    rest = jnp.concatenate([y[f * COLS + 128 : (f + 1) * COLS] for f in range(2)], axis=0)
    store(64, dot(tail, stack_lanes(rest.astype(BF))).astype(BF).reshape(16, 16, 128))


def silu(v):
    return v / (1.0 + jnp.exp(-v))


def spread(x, store):
    wide = x.astype(F32)
    i, _ = iotas(COLS, CH)
    before = jnp.where(i == 0, 0.0, pltpu.roll(wide, 1, 0))
    after = jnp.where(i == COLS - 1, 0.0, pltpu.roll(wide, COLS - 1, 0))
    store(0, x)
    store(1, before.astype(BF))
    store(2, after.astype(BF))


def spread_into(ref, first, x):
    def store(b, v):
        ref[pl.ds(first, COLS), pl.ds(b * CH, CH)] = v

    spread(x, store)


def conv_inner_kernel(
    x_ref, w_any, out_ref, edge_ref, outer_ref, xs, pay, pay_sum, mid_tap, sem, sems
):
    taps = (outer_ref.at[0], mid_tap, outer_ref.at[1])
    order = [(a, b) for a in (1, 2, 0) for b in (1, 0, 2)]
    spot = (1, 0, 2)
    weights = fetch(
        [w_any.at[a, pl.ds(b * CH, CH)] for a, b in order],
        [taps[a].at[pl.ds(spot[b] * CH, CH)] for a, b in order],
        sems,
    )
    weights[0].wait()
    centre = []
    for r in range(4):
        x = jnp.concatenate([x_ref[0, r], x_ref[1, r]], axis=0)
        centre.append(dot(x, mid_tap[pl.ds(0, CH), :]))
    edge_ref[0] = centre[0]
    edge_ref[1] = centre[3]
    for n in range(2):
        pay_sum[n] = centre[1 + n]
    for r in range(4):
        for f in range(2):
            spread_into(xs, r * PAIR + f * COLS, x_ref[f, r])
    tail = tail_matrix()

    def tap(r, a):
        return dot(xs[pl.ds((r + a - 1) * PAIR, PAIR), :], taps[a][...])

    def sides(r):
        return dot(xs[pl.ds(r * PAIR, PAIR), pl.ds(CH, 2 * CH)], mid_tap[pl.ds(CH, 2 * CH), :])

    for copy in weights[1:6]:
        copy.wait()
    edge_ref[0] = edge_ref[0] + sides(0) + tap(0, 2)
    for copy in weights[6:]:
        copy.wait()
    for r in (1, 2):
        y = silu(pay_sum[r - 1] + sides(r) + tap(r, 0) + tap(r, 2))

        def store(first, tiles, r=r):
            pay[pl.ds((r - 1) * 16, 16), pl.ds(first, 16), :] = tiles

        pack_row(y, tail, store)
    copy = pltpu.make_async_copy(pay, out_ref.at[pl.ds(16, 32)], sem)
    copy.start()
    edge_ref[1] = edge_ref[1] + sides(3) + tap(3, 0)
    copy.wait()


def conv_edge_kernel(first_ref, second_ref, edge_ref, w_ref, held_ref, out_ref, xs, pay, sem):
    del held_ref
    even = lax.axis_index("slab") % 2 == 0
    for f in range(2):
        first, second = first_ref[f, 0].astype(F32), second_ref[f, 0].astype(F32)
        spread_into(xs, f * COLS, jnp.where(even, second, first).astype(BF))
        spread_into(xs, PAIR + f * COLS, jnp.where(even, first, second).astype(BF))
    tail = tail_matrix()
    copies = []
    for n in range(2):
        y = silu(edge_ref[n] + dot(xs[pl.ds(n * PAIR, PAIR), :], w_ref[n]))

        def store(first, tiles, n=n):
            pay[n, :, pl.ds(first, 16), :] = tiles

        pack_row(y, tail, store)
        copies.append(
            pltpu.make_async_copy(pay.at[n], out_ref.at[pl.ds(48 * n, 16)], sem.at[n])
        )
        copies[n].start()
    for copy in copies:
        copy.wait()


def conv(latents, first, second, w_space):
    taps = far(w_space.reshape(3, 3 * CH, CH))
    payload = jax.ShapeDtypeStruct((64, 80, 128), BF)
    started, edge, outer = pl.pallas_call(
        conv_inner_kernel,
        out_shape=(
            payload,
            jax.ShapeDtypeStruct((2, PAIR, CH), F32),
            jax.ShapeDtypeStruct((2, 3 * CH, CH), BF),
        ),
        in_specs=[VMEM, HBM],
        out_specs=(ANY, VMEM, VMEM),
        scratch_shapes=[
            pltpu.VMEM((4 * PAIR, 3 * CH), BF),
            pltpu.VMEM((32, 80, 128), BF),
            pltpu.VMEM((2, PAIR, CH), F32),
            pltpu.VMEM((3 * CH, CH), BF),
            pltpu.SemaphoreType.DMA,
            pltpu.SemaphoreType.DMA((9,)),
        ],
        compiler_params=PARAMS,
        cost_estimate=pl.CostEstimate(
            flops=2 * 10 * PAIR * 3 * CH * CH, bytes_accessed=10 << 20, transcendentals=0
        ),
        name="conv_inner",
    )(latents, taps)
    return pl.pallas_call(
        conv_edge_kernel,
        out_shape=payload,
        in_specs=[VMEM, VMEM, VMEM, VMEM, ANY],
        out_specs=ANY,
        scratch_shapes=[
            pltpu.VMEM((2 * PAIR, 3 * CH), BF),
            pltpu.VMEM((2, 16, 80, 128), BF),
            pltpu.SemaphoreType.DMA((2,)),
        ],
        input_output_aliases={4: 0},
        compiler_params=PARAMS,
        name="conv_edge",
    )(first, second, edge, outer, started)


def gather_a(i):
    return ((i >> 1) & 7) * 16 + (i & 1) * 8 + (i >> 4)


def gather_b(i):
    return ((i >> 1) & 7) * 16 + (i >> 5) * 4 + ((i >> 4) & 1) * 2 + (i & 1)


def fetch(sources, buffers, sems):
    copies = [
        pltpu.make_async_copy(source, buffer, sems.at[n])
        for n, (source, buffer) in enumerate(zip(sources, buffers))
    ]
    for copy in copies:
        copy.start()
    return copies


def middle_kernel(
    x_ref, shift_ref, bias_ref, wt_any, wq_any, wo_any, out_ref,
    xs, mixed, qkv, att, res, wt_ref, wq_ref, wo_ref, sems,
):
    weights = fetch((wt_any, wq_any, wo_any), (wt_ref, wq_ref, wo_ref), sems)
    i, j = iotas(128, 128)
    take_a, take_b = one_hot(gather_a(i) == j), one_hot(gather_b(i) == j)
    give_a, give_b = one_hot(gather_a(j) == i), one_hot(gather_b(j) == i)
    for n in range(8):
        part = jnp.concatenate(
            [x_ref[pl.ds(8 * n, 8), pl.ds(16 * l, 16), :].reshape(128, 128) for l in range(4)],
            axis=1,
        )
        rows = dot(take_a, part).astype(BF)
        for k in range(8):
            xs[pl.ds(k * TOTAL + 16 * n, 16), pl.ds(0, CH)] = rows[16 * k : 16 * k + 16]
        rows = dot(take_b, x_ref[pl.ds(8 * n, 8), pl.ds(64, 16), :].reshape(128, 128)).astype(BF)
        for l in range(4):
            for k in range(2):
                at = (2 * l + k) * 16
                xs[pl.ds((8 + k) * TOTAL + 16 * n, 16), pl.ds(128 * l, 128)] = rows[at : at + 16]
    shift = shift_ref[...]
    for k in range(10):
        moved = dot(shift, xs[pl.ds(k * TOTAL, TOTAL), pl.ds(0, CH)]).astype(BF)
        xs[pl.ds(k * TOTAL, TOTAL), pl.ds(CH, CH)] = moved[:TOTAL]
        xs[pl.ds(k * TOTAL, TOTAL), pl.ds(2 * CH, CH)] = moved[TOTAL:]
    weights[0].wait()
    for c in range(2):
        part = pl.ds(640 * c, 640)
        mixed[part, :] = dot(xs[part, :], wt_ref[...]).astype(BF)
    weights[1].wait()
    for c in range(2):
        part = pl.ds(640 * c, 640)
        for t in range(3):
            cut = pl.ds(t * CH, CH)
            qkv[part, cut] = dot(mixed[part, :], wq_ref[:, cut]).astype(BF)

    bias = bias_ref[...]
    _, lane = iotas(TOTAL, 128)
    left = jnp.where(lane < 64, 1.0, 0.0).astype(BF)
    right = jnp.where(lane < 64, 0.0, 1.0).astype(BF)
    scale = BF(0.125)
    weigh = jnp.concatenate([left, right], axis=0)

    def pixel(k, carry):
        rows = pl.ds(pl.multiple_of(k * TOTAL, TOTAL), TOTAL)
        for h in range(4):
            q = qkv[rows, pl.ds(128 * h, 128)]
            key = qkv[rows, pl.ds(CH + 128 * h, 128)]
            v = qkv[rows, pl.ds(2 * CH + 128 * h, 128)]
            keys = jnp.concatenate([key * (left * scale), key * (right * scale)], axis=0)
            s = dot_t(q, keys)
            p = []
            for t in range(2):
                part = lanes(s, t) + bias
                p.append(jnp.exp(part - jnp.max(part, axis=-1, keepdims=True)).astype(BF))
            values = jnp.concatenate([jnp.concatenate([v * left, v * right], axis=0), weigh], axis=1)
            o = dot(jnp.concatenate(p, axis=1), values)
            att[rows, pl.ds(128 * h, 128)] = (o[:, :128] / o[:, 128:]).astype(BF)
        return carry

    lax.fori_loop(0, 10, pixel, 0, unroll=10)
    weights[2].wait()
    for c in range(2):
        part = pl.ds(640 * c, 640)
        res[part, :] = dot(att[part, :], wo_ref[...]).astype(BF)
    for n in range(8):
        rows = jnp.concatenate(
            [res[pl.ds(k * TOTAL + 16 * n, 16), :] for k in range(8)], axis=0
        )
        part = dot(give_a, rows).astype(BF)
        for l in range(4):
            out_ref[pl.ds(8 * n, 8), pl.ds(16 * l, 16), :] = lanes(part, l).reshape(8, 16, 128)
        rows = jnp.concatenate(
            [
                res[pl.ds((8 + k) * TOTAL + 16 * n, 16), pl.ds(128 * l, 128)]
                for l in range(4)
                for k in range(2)
            ],
            axis=0,
        )
        out_ref[pl.ds(8 * n, 8), pl.ds(64, 16), :] = dot(give_b, rows).astype(BF).reshape(8, 16, 128)


def middle(arrived, clip_starts, w_time, w_qkv, w_out):
    clip_ids = jnp.cumsum(clip_starts)
    same = clip_ids[None, :] == clip_ids[:, None]
    i, j = iotas(TOTAL, TOTAL)
    bias = jnp.where(same & (j <= i), 0.0, -1e30).astype(F32)
    shift = jnp.concatenate([one_hot(same & (j == i - 1)), one_hot(same & (j == i - 2))], axis=0)
    return pl.pallas_call(
        middle_kernel,
        out_shape=jax.ShapeDtypeStruct((64, 80, 128), BF),
        in_specs=[VMEM] * 3 + [HBM] * 3,
        out_specs=VMEM,
        scratch_shapes=[
            pltpu.VMEM((1280, 3 * CH), BF),
            pltpu.VMEM((1280, CH), BF),
            pltpu.VMEM((1280, 3 * CH), BF),
            pltpu.VMEM((1280, CH), BF),
            pltpu.VMEM((1280, CH), BF),
            pltpu.VMEM((3 * CH, CH), BF),
            pltpu.VMEM((CH, 3 * CH), BF),
            pltpu.VMEM((CH, CH), BF),
            pltpu.SemaphoreType.DMA((3,)),
        ],
        compiler_params=PARAMS,
        name="middle",
    )(arrived, shift, bias, far(w_time.reshape(3 * CH, CH)), far(w_qkv), far(w_out))


def finish_kernel(x_ref, latent_ref, out_any, out, sems):
    i, j = iotas(256, 256)
    spread_tail = one_hot(tail_source(j) == i)
    copies = []
    for r in range(4):
        part = pl.ds(16 * r, 16)
        head = [x_ref[part, pl.ds(16 * l, 16), :].astype(F32) for l in range(4)]
        rest = dot(spread_tail, x_ref[part, pl.ds(64, 16), :].reshape(256, 128))
        for f in range(2):
            for l in range(4):
                cut = pl.ds(128 * l, 128)
                add = head[l][:, 8 * f : 8 * f + 8].reshape(128, 128)
                old = latent_ref[f, r, pl.ds(0, 128), cut].astype(F32)
                out[r, f, pl.ds(0, 128), cut] = (old + add).astype(BF)
                at = 64 * l + 32 * f
                old = latent_ref[f, r, pl.ds(128, 32), cut].astype(F32)
                out[r, f, pl.ds(128, 32), cut] = (old + rest[at : at + 32]).astype(BF)
        copies.append(pltpu.make_async_copy(out.at[r], out_any.at[:, r], sems.at[r]))
        copies[r].start()
    for copy in copies:
        copy.wait()


def finish(returned, latents):
    return pl.pallas_call(
        finish_kernel,
        out_shape=jax.ShapeDtypeStruct(latents.shape, BF),
        in_specs=[VMEM, VMEM],
        out_specs=ANY,
        scratch_shapes=[pltpu.VMEM((4, 2, COLS, CH), BF), pltpu.SemaphoreType.DMA((4,))],
        compiler_params=PARAMS,
        name="finish",
    )(returned, latents)


def swap(x, lower):
    return lax.ppermute(x, "slab", [p for i in lower for p in ((i, i + 1), (i + 1, i))])


def on_device(latents, clip_starts, w_space, w_time, w_qkv, w_out):
    count = lax.axis_size("slab")
    even = lax.axis_index("slab") % 2 == 0
    top, bottom = latents[:, :1], latents[:, 3:]
    first = swap(jnp.where(even, bottom, top), range(0, count - 1, 2))
    second = swap(jnp.where(even, top, bottom), range(1, count - 1, 2))
    payload = conv(latents, first, second, w_space)
    arrived = lax.all_to_all(payload, FRAME, split_axis=0, concat_axis=0, tiled=True)
    result = middle(arrived, clip_starts, w_time, w_qkv, w_out)
    returned = lax.all_to_all(result, FRAME, split_axis=0, concat_axis=0, tiled=True)
    return finish(returned, latents)


def solution(mesh):
    finer = Mesh(
        mesh.devices.reshape(8, 4, 2, mesh.shape["slab"]), ("frame_0", "frame_1", "frame_2", "slab")
    )
    return jax.shard_map(
        on_device,
        mesh=finer,
        in_specs=(P(FRAME, "slab", None, None), P(), P(), P(), P(), P()),
        out_specs=P(FRAME, "slab", None, None),
        check_vma=False,
    )
```

```python
import functools

import jax
import jax.numpy as jnp
from jax import lax
from jax.experimental import pallas as pl
from jax.experimental.pallas import tpu as pltpu
from jax.sharding import Mesh
from jax.sharding import PartitionSpec as P

HEADS = 8
FRAME = ("frame_0", "frame_1", "frame_2")
BF = jnp.bfloat16
F32 = jnp.float32
COLS = 160
CH = 512
PAIR = 2 * COLS
TOTAL = 128
VMEM = pl.BlockSpec(memory_space=pltpu.VMEM)
ANY = pl.BlockSpec(memory_space=pl.ANY)
HBM = pl.BlockSpec(memory_space=pltpu.HBM)


def far(x):
    return pltpu.with_memory_space_constraint(x, pltpu.HBM)
PARAMS = pltpu.CompilerParams(vmem_limit_bytes=20 * 1024 * 1024)


def dot(a, b):
    return jnp.dot(a, b, preferred_element_type=F32)


def dot_t(a, b):
    return lax.dot_general(a, b, (((1,), (1,)), ((), ())), preferred_element_type=F32)


def iotas(rows, cols):
    i = lax.broadcasted_iota(jnp.int32, (rows, cols), 0)
    j = lax.broadcasted_iota(jnp.int32, (rows, cols), 1)
    return i, j


def one_hot(hit):
    return jnp.where(hit, 1.0, 0.0).astype(BF)


def tail_source(i):
    return ((i >> 2) & 3) * 64 + (i & 1) * 32 + 2 * (i >> 4) + ((i >> 1) & 1)


def lanes(x, l):
    return x[:, l * 128 : (l + 1) * 128]


def stack_lanes(x):
    return jnp.concatenate([lanes(x, l) for l in range(4)], axis=0)


def tail_matrix():
    i, j = iotas(256, 256)
    return one_hot(tail_source(i) == j)


def pack_row(y, tail, store):
    halves = [y[f * COLS : f * COLS + 128].reshape(16, 8, CH) for f in range(2)]
    head = jnp.concatenate(halves, axis=1).astype(BF)
    for l in range(4):
        store(16 * l, head[:, :, l * 128 : (l + 1) * 128])
    rest = jnp.concatenate([y[f * COLS + 128 : (f + 1) * COLS] for f in range(2)], axis=0)
    store(64, dot(tail, stack_lanes(rest.astype(BF))).astype(BF).reshape(16, 16, 128))


def silu(v):
    return v / (1.0 + jnp.exp(-v))


def spread(x, store):
    wide = x.astype(F32)
    i, _ = iotas(COLS, CH)
    before = jnp.where(i == 0, 0.0, pltpu.roll(wide, 1, 0))
    after = jnp.where(i == COLS - 1, 0.0, pltpu.roll(wide, COLS - 1, 0))
    store(0, x)
    store(1, before.astype(BF))
    store(2, after.astype(BF))


def spread_into(ref, first, x):
    def store(b, v):
        ref[pl.ds(first, COLS), pl.ds(b * CH, CH)] = v

    spread(x, store)


def conv_inner_kernel(
    x_ref, w_any, out_ref, edge_ref, outer_ref, xs, pay, pay_sum, mid_tap, sem, sems
):
    taps = (outer_ref.at[0], mid_tap, outer_ref.at[1])
    order = [(a, b) for a in (1, 2, 0) for b in (1, 0, 2)]
    spot = (1, 0, 2)
    weights = fetch(
        [w_any.at[a, pl.ds(b * CH, CH)] for a, b in order],
        [taps[a].at[pl.ds(spot[b] * CH, CH)] for a, b in order],
        sems,
    )
    weights[0].wait()
    centre = []
    for r in range(4):
        x = jnp.concatenate([x_ref[0, r], x_ref[1, r]], axis=0)
        centre.append(dot(x, mid_tap[pl.ds(0, CH), :]))
    edge_ref[0] = centre[0]
    edge_ref[1] = centre[3]
    for n in range(2):
        pay_sum[n] = centre[1 + n]
    for r in range(4):
        for f in range(2):
            spread_into(xs, r * PAIR + f * COLS, x_ref[f, r])
    tail = tail_matrix()

    def tap(r, a):
        return dot(xs[pl.ds((r + a - 1) * PAIR, PAIR), :], taps[a][...])

    def sides(r):
        return dot(xs[pl.ds(r * PAIR, PAIR), pl.ds(CH, 2 * CH)], mid_tap[pl.ds(CH, 2 * CH), :])

    for copy in weights[1:6]:
        copy.wait()
    edge_ref[0] = edge_ref[0] + sides(0) + tap(0, 2)
    for copy in weights[6:]:
        copy.wait()
    for r in (1, 2):
        y = silu(pay_sum[r - 1] + sides(r) + tap(r, 0) + tap(r, 2))

        def store(first, tiles, r=r):
            pay[pl.ds((r - 1) * 16, 16), pl.ds(first, 16), :] = tiles

        pack_row(y, tail, store)
    copy = pltpu.make_async_copy(pay, out_ref.at[pl.ds(16, 32)], sem)
    copy.start()
    edge_ref[1] = edge_ref[1] + sides(3) + tap(3, 0)
    copy.wait()


def conv_edge_kernel(first_ref, second_ref, edge_ref, w_ref, held_ref, out_ref, xs, pay, sem):
    del held_ref
    even = lax.axis_index("slab") % 2 == 0
    for f in range(2):
        first, second = first_ref[f, 0].astype(F32), second_ref[f, 0].astype(F32)
        spread_into(xs, f * COLS, jnp.where(even, second, first).astype(BF))
        spread_into(xs, PAIR + f * COLS, jnp.where(even, first, second).astype(BF))
    tail = tail_matrix()
    copies = []
    for n in range(2):
        y = silu(edge_ref[n] + dot(xs[pl.ds(n * PAIR, PAIR), :], w_ref[n]))

        def store(first, tiles, n=n):
            pay[n, :, pl.ds(first, 16), :] = tiles

        pack_row(y, tail, store)
        copies.append(
            pltpu.make_async_copy(pay.at[n], out_ref.at[pl.ds(48 * n, 16)], sem.at[n])
        )
        copies[n].start()
    for copy in copies:
        copy.wait()


def conv(latents, first, second, w_space):
    taps = far(w_space.reshape(3, 3 * CH, CH))
    payload = jax.ShapeDtypeStruct((64, 80, 128), BF)
    started, edge, outer = pl.pallas_call(
        conv_inner_kernel,
        out_shape=(
            payload,
            jax.ShapeDtypeStruct((2, PAIR, CH), F32),
            jax.ShapeDtypeStruct((2, 3 * CH, CH), BF),
        ),
        in_specs=[VMEM, HBM],
        out_specs=(ANY, VMEM, VMEM),
        scratch_shapes=[
            pltpu.VMEM((4 * PAIR, 3 * CH), BF),
            pltpu.VMEM((32, 80, 128), BF),
            pltpu.VMEM((2, PAIR, CH), F32),
            pltpu.VMEM((3 * CH, CH), BF),
            pltpu.SemaphoreType.DMA,
            pltpu.SemaphoreType.DMA((9,)),
        ],
        compiler_params=PARAMS,
        cost_estimate=pl.CostEstimate(
            flops=2 * 10 * PAIR * 3 * CH * CH, bytes_accessed=10 << 20, transcendentals=0
        ),
        name="conv_inner",
    )(latents, taps)
    return pl.pallas_call(
        conv_edge_kernel,
        out_shape=payload,
        in_specs=[VMEM, VMEM, VMEM, VMEM, ANY],
        out_specs=ANY,
        scratch_shapes=[
            pltpu.VMEM((2 * PAIR, 3 * CH), BF),
            pltpu.VMEM((2, 16, 80, 128), BF),
            pltpu.SemaphoreType.DMA((2,)),
        ],
        input_output_aliases={4: 0},
        compiler_params=PARAMS,
        name="conv_edge",
    )(first, second, edge, outer, started)


def gather_a(i):
    return ((i >> 1) & 7) * 16 + (i & 1) * 8 + (i >> 4)


def gather_b(i):
    return ((i >> 1) & 7) * 16 + (i >> 5) * 4 + ((i >> 4) & 1) * 2 + (i & 1)


def fetch(sources, buffers, sems):
    copies = [
        pltpu.make_async_copy(source, buffer, sems.at[n])
        for n, (source, buffer) in enumerate(zip(sources, buffers))
    ]
    for copy in copies:
        copy.start()
    return copies


def middle_kernel(
    x_ref, shift_ref, bias_ref, wt_any, wq_any, wo_any, out_ref,
    xs, mixed, qkv, att, res, wt_ref, wq_ref, wo_ref, sems,
):
    weights = fetch((wt_any, wq_any, wo_any), (wt_ref, wq_ref, wo_ref), sems)
    i, j = iotas(128, 128)
    take_a, take_b = one_hot(gather_a(i) == j), one_hot(gather_b(i) == j)
    give_a, give_b = one_hot(gather_a(j) == i), one_hot(gather_b(j) == i)
    for n in range(8):
        part = jnp.concatenate(
            [x_ref[pl.ds(8 * n, 8), pl.ds(16 * l, 16), :].reshape(128, 128) for l in range(4)],
            axis=1,
        )
        rows = dot(take_a, part).astype(BF)
        for k in range(8):
            xs[pl.ds(k * TOTAL + 16 * n, 16), pl.ds(0, CH)] = rows[16 * k : 16 * k + 16]
        rows = dot(take_b, x_ref[pl.ds(8 * n, 8), pl.ds(64, 16), :].reshape(128, 128)).astype(BF)
        for l in range(4):
            for k in range(2):
                at = (2 * l + k) * 16
                xs[pl.ds((8 + k) * TOTAL + 16 * n, 16), pl.ds(128 * l, 128)] = rows[at : at + 16]
    shift = shift_ref[...]
    for k in range(10):
        moved = dot(shift, xs[pl.ds(k * TOTAL, TOTAL), pl.ds(0, CH)]).astype(BF)
        xs[pl.ds(k * TOTAL, TOTAL), pl.ds(CH, CH)] = moved[:TOTAL]
        xs[pl.ds(k * TOTAL, TOTAL), pl.ds(2 * CH, CH)] = moved[TOTAL:]
    weights[0].wait()
    for c in range(2):
        part = pl.ds(640 * c, 640)
        mixed[part, :] = dot(xs[part, :], wt_ref[...]).astype(BF)
    weights[1].wait()
    for c in range(2):
        part = pl.ds(640 * c, 640)
        for t in range(3):
            cut = pl.ds(t * CH, CH)
            qkv[part, cut] = dot(mixed[part, :], wq_ref[:, cut]).astype(BF)

    bias = bias_ref[...]
    _, lane = iotas(TOTAL, 128)
    left = jnp.where(lane < 64, 1.0, 0.0).astype(BF)
    right = jnp.where(lane < 64, 0.0, 1.0).astype(BF)
    scale = BF(0.125)
    weigh = jnp.concatenate([left, right], axis=0)

    def pixel(k, carry):
        rows = pl.ds(pl.multiple_of(k * TOTAL, TOTAL), TOTAL)
        for h in range(4):
            q = qkv[rows, pl.ds(128 * h, 128)]
            key = qkv[rows, pl.ds(CH + 128 * h, 128)]
            v = qkv[rows, pl.ds(2 * CH + 128 * h, 128)]
            keys = jnp.concatenate([key * (left * scale), key * (right * scale)], axis=0)
            s = dot_t(q, keys)
            p = []
            for t in range(2):
                part = lanes(s, t) + bias
                p.append(jnp.exp(part - jnp.max(part, axis=-1, keepdims=True)).astype(BF))
            values = jnp.concatenate([jnp.concatenate([v * left, v * right], axis=0), weigh], axis=1)
            o = dot(jnp.concatenate(p, axis=1), values)
            att[rows, pl.ds(128 * h, 128)] = (o[:, :128] / o[:, 128:]).astype(BF)
        return carry

    lax.fori_loop(0, 10, pixel, 0, unroll=10)
    weights[2].wait()
    for c in range(2):
        part = pl.ds(640 * c, 640)
        res[part, :] = dot(att[part, :], wo_ref[...]).astype(BF)
    for n in range(8):
        rows = jnp.concatenate(
            [res[pl.ds(k * TOTAL + 16 * n, 16), :] for k in range(8)], axis=0
        )
        part = dot(give_a, rows).astype(BF)
        for l in range(4):
            out_ref[pl.ds(8 * n, 8), pl.ds(16 * l, 16), :] = lanes(part, l).reshape(8, 16, 128)
        rows = jnp.concatenate(
            [
                res[pl.ds((8 + k) * TOTAL + 16 * n, 16), pl.ds(128 * l, 128)]
                for l in range(4)
                for k in range(2)
            ],
            axis=0,
        )
        out_ref[pl.ds(8 * n, 8), pl.ds(64, 16), :] = dot(give_b, rows).astype(BF).reshape(8, 16, 128)


def middle(arrived, clip_starts, w_time, w_qkv, w_out):
    clip_ids = jnp.cumsum(clip_starts)
    same = clip_ids[None, :] == clip_ids[:, None]
    i, j = iotas(TOTAL, TOTAL)
    bias = jnp.where(same & (j <= i), 0.0, -1e30).astype(F32)
    shift = jnp.concatenate([one_hot(same & (j == i - 1)), one_hot(same & (j == i - 2))], axis=0)
    return pl.pallas_call(
        middle_kernel,
        out_shape=jax.ShapeDtypeStruct((64, 80, 128), BF),
        in_specs=[VMEM] * 3 + [HBM] * 3,
        out_specs=VMEM,
        scratch_shapes=[
            pltpu.VMEM((1280, 3 * CH), BF),
            pltpu.VMEM((1280, CH), BF),
            pltpu.VMEM((1280, 3 * CH), BF),
            pltpu.VMEM((1280, CH), BF),
            pltpu.VMEM((1280, CH), BF),
            pltpu.VMEM((3 * CH, CH), BF),
            pltpu.VMEM((CH, 3 * CH), BF),
            pltpu.VMEM((CH, CH), BF),
            pltpu.SemaphoreType.DMA((3,)),
        ],
        compiler_params=pltpu.CompilerParams(
            vmem_limit_bytes=20 * 1024 * 1024
        ),
        name="middle",
    )(arrived, shift, bias, far(w_time.reshape(3 * CH, CH)), far(w_qkv), far(w_out))


def finish_kernel(x_ref, latent_ref, out_any, out, sems):
    i, j = iotas(256, 256)
    spread_tail = one_hot(tail_source(j) == i)
    copies = []
    for r in range(4):
        part = pl.ds(16 * r, 16)
        head = [x_ref[part, pl.ds(16 * l, 16), :].astype(F32) for l in range(4)]
        rest = dot(spread_tail, x_ref[part, pl.ds(64, 16), :].reshape(256, 128))
        for f in range(2):
            for l in range(4):
                cut = pl.ds(128 * l, 128)
                add = head[l][:, 8 * f : 8 * f + 8].reshape(128, 128)
                old = latent_ref[f, r, pl.ds(0, 128), cut].astype(F32)
                out[r, f, pl.ds(0, 128), cut] = (old + add).astype(BF)
                at = 64 * l + 32 * f
                old = latent_ref[f, r, pl.ds(128, 32), cut].astype(F32)
                out[r, f, pl.ds(128, 32), cut] = (old + rest[at : at + 32]).astype(BF)
        copies.append(pltpu.make_async_copy(out.at[r], out_any.at[:, r], sems.at[r]))
        copies[r].start()
    for copy in copies:
        copy.wait()


def finish(returned, latents):
    return pl.pallas_call(
        finish_kernel,
        out_shape=jax.ShapeDtypeStruct(latents.shape, BF),
        in_specs=[VMEM, VMEM],
        out_specs=ANY,
        scratch_shapes=[pltpu.VMEM((4, 2, COLS, CH), BF), pltpu.SemaphoreType.DMA((4,))],
        compiler_params=PARAMS,
        name="finish",
    )(returned, latents)


def swap(x, lower):
    return lax.ppermute(x, "slab", [p for i in lower for p in ((i, i + 1), (i + 1, i))])


def on_device(latents, clip_starts, w_space, w_time, w_qkv, w_out):
    count = lax.axis_size("slab")
    even = lax.axis_index("slab") % 2 == 0
    top, bottom = latents[:, :1], latents[:, 3:]
    first = swap(jnp.where(even, bottom, top), range(0, count - 1, 2))
    second = swap(jnp.where(even, top, bottom), range(1, count - 1, 2))
    payload = conv(latents, first, second, w_space)
    arrived = lax.all_to_all(payload, FRAME, split_axis=0, concat_axis=0, tiled=True)
    result = middle(arrived, clip_starts, w_time, w_qkv, w_out)
    returned = lax.all_to_all(result, FRAME, split_axis=0, concat_axis=0, tiled=True)
    return finish(returned, latents)


def solution(mesh):
    finer = Mesh(
        mesh.devices.reshape(8, 4, 2, mesh.shape["slab"]), ("frame_0", "frame_1", "frame_2", "slab")
    )
    return jax.shard_map(
        on_device,
        mesh=finer,
        in_specs=(P(FRAME, "slab", None, None), P(), P(), P(), P(), P()),
        out_specs=P(FRAME, "slab", None, None),
        check_vma=False,
    )
```

```python
import functools

import jax
import jax.numpy as jnp
from jax import lax
from jax.experimental import pallas as pl
from jax.experimental.pallas import tpu as pltpu
from jax.sharding import Mesh
from jax.sharding import PartitionSpec as P

HEADS = 8
FRAME = ("frame_0", "frame_1", "frame_2")
BF = jnp.bfloat16
F32 = jnp.float32
COLS = 160
CH = 512
PAIR = 2 * COLS
TOTAL = 128
VMEM = pl.BlockSpec(memory_space=pltpu.VMEM)
ANY = pl.BlockSpec(memory_space=pl.ANY)
HBM = pl.BlockSpec(memory_space=pltpu.HBM)


def far(x):
    return pltpu.with_memory_space_constraint(x, pltpu.HBM)
PARAMS = pltpu.CompilerParams(vmem_limit_bytes=20 * 1024 * 1024)


def dot(a, b):
    return jnp.dot(a, b, preferred_element_type=F32)


def dot_t(a, b):
    return lax.dot_general(a, b, (((1,), (1,)), ((), ())), preferred_element_type=F32)


def iotas(rows, cols):
    i = lax.broadcasted_iota(jnp.int32, (rows, cols), 0)
    j = lax.broadcasted_iota(jnp.int32, (rows, cols), 1)
    return i, j


def one_hot(hit):
    return jnp.where(hit, 1.0, 0.0).astype(BF)


def tail_source(i):
    return ((i >> 2) & 3) * 64 + (i & 1) * 32 + 2 * (i >> 4) + ((i >> 1) & 1)


def lanes(x, l):
    return x[:, l * 128 : (l + 1) * 128]


def stack_lanes(x):
    return jnp.concatenate([lanes(x, l) for l in range(4)], axis=0)


def tail_matrix():
    i, j = iotas(256, 256)
    return one_hot(tail_source(i) == j)


def pack_row(y, tail, store):
    halves = [y[f * COLS : f * COLS + 128].reshape(16, 8, CH) for f in range(2)]
    head = jnp.concatenate(halves, axis=1).astype(BF)
    for l in range(4):
        store(16 * l, head[:, :, l * 128 : (l + 1) * 128])
    rest = jnp.concatenate([y[f * COLS + 128 : (f + 1) * COLS] for f in range(2)], axis=0)
    store(64, dot(tail, stack_lanes(rest.astype(BF))).astype(BF).reshape(16, 16, 128))


def silu(v):
    return v / (1.0 + jnp.exp(-v))


def spread(x, store):
    wide = x.astype(F32)
    i, _ = iotas(COLS, CH)
    before = jnp.where(i == 0, 0.0, pltpu.roll(wide, 1, 0))
    after = jnp.where(i == COLS - 1, 0.0, pltpu.roll(wide, COLS - 1, 0))
    store(0, x)
    store(1, before.astype(BF))
    store(2, after.astype(BF))


def spread_into(ref, first, x):
    def store(b, v):
        ref[pl.ds(first, COLS), pl.ds(b * CH, CH)] = v

    spread(x, store)


def conv_inner_kernel(
    x_ref, w_any, out_ref, edge_ref, outer_ref, xs, pay, pay_sum, mid_tap, sem, sems
):
    taps = (outer_ref.at[0], mid_tap, outer_ref.at[1])
    order = [(a, b) for a in (1, 2, 0) for b in (1, 0, 2)]
    spot = (1, 0, 2)
    weights = fetch(
        [w_any.at[a, pl.ds(b * CH, CH)] for a, b in order],
        [taps[a].at[pl.ds(spot[b] * CH, CH)] for a, b in order],
        sems,
    )
    for r in range(0, 4):
        for f in range(2):
            spread_into(xs, r * PAIR + f * COLS, x_ref[f, r])
    weights[0].wait()
    centre = []
    for r in range(4):
        x = jnp.concatenate([x_ref[0, r], x_ref[1, r]], axis=0)
        centre.append(dot(x, mid_tap[pl.ds(0, CH), :]))
    edge_ref[0] = centre[0]
    edge_ref[1] = centre[3]
    for n in range(2):
        pay_sum[n] = centre[1 + n]
    tail = tail_matrix()

    def tap(r, a):
        return dot(xs[pl.ds((r + a - 1) * PAIR, PAIR), :], taps[a][...])

    def sides(r):
        return dot(xs[pl.ds(r * PAIR, PAIR), pl.ds(CH, 2 * CH)], mid_tap[pl.ds(CH, 2 * CH), :])

    for copy in weights[1:6]:
        copy.wait()
    edge_ref[0] = edge_ref[0] + sides(0) + tap(0, 2)
    for copy in weights[6:]:
        copy.wait()
    for r in (1, 2):
        y = silu(pay_sum[r - 1] + sides(r) + tap(r, 0) + tap(r, 2))

        def store(first, tiles, r=r):
            pay[pl.ds((r - 1) * 16, 16), pl.ds(first, 16), :] = tiles

        pack_row(y, tail, store)
    copy = pltpu.make_async_copy(pay, out_ref.at[pl.ds(16, 32)], sem)
    copy.start()
    edge_ref[1] = edge_ref[1] + sides(3) + tap(3, 0)
    copy.wait()


def conv_edge_kernel(first_ref, second_ref, edge_ref, w_ref, held_ref, out_ref, xs, pay, sem):
    del held_ref
    even = lax.axis_index("slab") % 2 == 0
    for f in range(2):
        first, second = first_ref[f, 0].astype(F32), second_ref[f, 0].astype(F32)
        spread_into(xs, f * COLS, jnp.where(even, second, first).astype(BF))
        spread_into(xs, PAIR + f * COLS, jnp.where(even, first, second).astype(BF))
    tail = tail_matrix()
    copies = []
    for n in range(2):
        y = silu(edge_ref[n] + dot(xs[pl.ds(n * PAIR, PAIR), :], w_ref[n]))

        def store(first, tiles, n=n):
            pay[n, :, pl.ds(first, 16), :] = tiles

        pack_row(y, tail, store)
        copies.append(
            pltpu.make_async_copy(pay.at[n], out_ref.at[pl.ds(48 * n, 16)], sem.at[n])
        )
        copies[n].start()
    for copy in copies:
        copy.wait()


def conv(latents, first, second, w_space):
    taps = far(w_space.reshape(3, 3 * CH, CH))
    payload = jax.ShapeDtypeStruct((64, 80, 128), BF)
    started, edge, outer = pl.pallas_call(
        conv_inner_kernel,
        out_shape=(
            payload,
            jax.ShapeDtypeStruct((2, PAIR, CH), F32),
            jax.ShapeDtypeStruct((2, 3 * CH, CH), BF),
        ),
        in_specs=[VMEM, HBM],
        out_specs=(ANY, VMEM, VMEM),
        scratch_shapes=[
            pltpu.VMEM((4 * PAIR, 3 * CH), BF),
            pltpu.VMEM((32, 80, 128), BF),
            pltpu.VMEM((2, PAIR, CH), F32),
            pltpu.VMEM((3 * CH, CH), BF),
            pltpu.SemaphoreType.DMA,
            pltpu.SemaphoreType.DMA((9,)),
        ],
        compiler_params=PARAMS,
        cost_estimate=pl.CostEstimate(
            flops=2 * 10 * PAIR * 3 * CH * CH, bytes_accessed=10 << 20, transcendentals=0
        ),
        name="conv_inner",
    )(latents, taps)
    return pl.pallas_call(
        conv_edge_kernel,
        out_shape=payload,
        in_specs=[VMEM, VMEM, VMEM, VMEM, ANY],
        out_specs=ANY,
        scratch_shapes=[
            pltpu.VMEM((2 * PAIR, 3 * CH), BF),
            pltpu.VMEM((2, 16, 80, 128), BF),
            pltpu.SemaphoreType.DMA((2,)),
        ],
        input_output_aliases={4: 0},
        compiler_params=PARAMS,
        name="conv_edge",
    )(first, second, edge, outer, started)


def gather_a(i):
    return ((i >> 1) & 7) * 16 + (i & 1) * 8 + (i >> 4)


def gather_b(i):
    return ((i >> 1) & 7) * 16 + (i >> 5) * 4 + ((i >> 4) & 1) * 2 + (i & 1)


def fetch(sources, buffers, sems):
    copies = [
        pltpu.make_async_copy(source, buffer, sems.at[n])
        for n, (source, buffer) in enumerate(zip(sources, buffers))
    ]
    for copy in copies:
        copy.start()
    return copies


def middle_kernel(
    x_ref, shift_ref, bias_ref, wt_any, wq_any, wo_any, out_ref,
    xs, mixed, qkv, att, res, wt_ref, wq_ref, wo_ref, sems,
):
    weights = fetch((wt_any, wq_any, wo_any), (wt_ref, wq_ref, wo_ref), sems)
    i, j = iotas(128, 128)
    take_a, take_b = one_hot(gather_a(i) == j), one_hot(gather_b(i) == j)
    give_a, give_b = one_hot(gather_a(j) == i), one_hot(gather_b(j) == i)
    for n in range(8):
        part = jnp.concatenate(
            [x_ref[pl.ds(8 * n, 8), pl.ds(16 * l, 16), :].reshape(128, 128) for l in range(4)],
            axis=1,
        )
        rows = dot(take_a, part).astype(BF)
        for k in range(8):
            xs[pl.ds(k * TOTAL + 16 * n, 16), pl.ds(0, CH)] = rows[16 * k : 16 * k + 16]
        rows = dot(take_b, x_ref[pl.ds(8 * n, 8), pl.ds(64, 16), :].reshape(128, 128)).astype(BF)
        for l in range(4):
            for k in range(2):
                at = (2 * l + k) * 16
                xs[pl.ds((8 + k) * TOTAL + 16 * n, 16), pl.ds(128 * l, 128)] = rows[at : at + 16]
    shift = shift_ref[...]
    for k in range(10):
        moved = dot(shift, xs[pl.ds(k * TOTAL, TOTAL), pl.ds(0, CH)]).astype(BF)
        xs[pl.ds(k * TOTAL, TOTAL), pl.ds(CH, CH)] = moved[:TOTAL]
        xs[pl.ds(k * TOTAL, TOTAL), pl.ds(2 * CH, CH)] = moved[TOTAL:]
    weights[0].wait()
    for c in range(2):
        part = pl.ds(640 * c, 640)
        mixed[part, :] = dot(xs[part, :], wt_ref[...]).astype(BF)
    weights[1].wait()
    for c in range(2):
        part = pl.ds(640 * c, 640)
        for t in range(3):
            cut = pl.ds(t * CH, CH)
            qkv[part, cut] = dot(mixed[part, :], wq_ref[:, cut]).astype(BF)

    bias = bias_ref[...]
    _, lane = iotas(TOTAL, 128)
    left = jnp.where(lane < 64, 1.0, 0.0).astype(BF)
    right = jnp.where(lane < 64, 0.0, 1.0).astype(BF)
    scale = BF(0.125)
    weigh = jnp.concatenate([left, right], axis=0)

    def pixel(k, carry):
        rows = pl.ds(pl.multiple_of(k * TOTAL, TOTAL), TOTAL)
        for h in range(4):
            q = qkv[rows, pl.ds(128 * h, 128)]
            key = qkv[rows, pl.ds(CH + 128 * h, 128)]
            v = qkv[rows, pl.ds(2 * CH + 128 * h, 128)]
            keys = jnp.concatenate([key * (left * scale), key * (right * scale)], axis=0)
            s = dot_t(q, keys)
            p = []
            for t in range(2):
                part = lanes(s, t) + bias
                p.append(jnp.exp(part - jnp.max(part, axis=-1, keepdims=True)).astype(BF))
            values = jnp.concatenate([jnp.concatenate([v * left, v * right], axis=0), weigh], axis=1)
            o = dot(jnp.concatenate(p, axis=1), values)
            att[rows, pl.ds(128 * h, 128)] = (o[:, :128] / o[:, 128:]).astype(BF)
        return carry

    lax.fori_loop(0, 10, pixel, 0, unroll=10)
    weights[2].wait()
    for c in range(2):
        part = pl.ds(640 * c, 640)
        res[part, :] = dot(att[part, :], wo_ref[...]).astype(BF)
    for n in range(8):
        rows = jnp.concatenate(
            [res[pl.ds(k * TOTAL + 16 * n, 16), :] for k in range(8)], axis=0
        )
        part = dot(give_a, rows).astype(BF)
        for l in range(4):
            out_ref[pl.ds(8 * n, 8), pl.ds(16 * l, 16), :] = lanes(part, l).reshape(8, 16, 128)
        rows = jnp.concatenate(
            [
                res[pl.ds((8 + k) * TOTAL + 16 * n, 16), pl.ds(128 * l, 128)]
                for l in range(4)
                for k in range(2)
            ],
            axis=0,
        )
        out_ref[pl.ds(8 * n, 8), pl.ds(64, 16), :] = dot(give_b, rows).astype(BF).reshape(8, 16, 128)


def middle(arrived, clip_starts, w_time, w_qkv, w_out):
    clip_ids = jnp.cumsum(clip_starts)
    same = clip_ids[None, :] == clip_ids[:, None]
    i, j = iotas(TOTAL, TOTAL)
    bias = jnp.where(same & (j <= i), 0.0, -1e30).astype(F32)
    shift = jnp.concatenate([one_hot(same & (j == i - 1)), one_hot(same & (j == i - 2))], axis=0)
    return pl.pallas_call(
        middle_kernel,
        out_shape=jax.ShapeDtypeStruct((64, 80, 128), BF),
        in_specs=[VMEM] * 3 + [HBM] * 3,
        out_specs=VMEM,
        scratch_shapes=[
            pltpu.VMEM((1280, 3 * CH), BF),
            pltpu.VMEM((1280, CH), BF),
            pltpu.VMEM((1280, 3 * CH), BF),
            pltpu.VMEM((1280, CH), BF),
            pltpu.VMEM((1280, CH), BF),
            pltpu.VMEM((3 * CH, CH), BF),
            pltpu.VMEM((CH, 3 * CH), BF),
            pltpu.VMEM((CH, CH), BF),
            pltpu.SemaphoreType.DMA((3,)),
        ],
        compiler_params=pltpu.CompilerParams(
            vmem_limit_bytes=20 * 1024 * 1024
        ),
        name="middle",
    )(arrived, shift, bias, far(w_time.reshape(3 * CH, CH)), far(w_qkv), far(w_out))


def finish_kernel(x_ref, latent_ref, out_any, out, sems):
    i, j = iotas(256, 256)
    spread_tail = one_hot(tail_source(j) == i)
    copies = []
    for r in range(4):
        part = pl.ds(16 * r, 16)
        head = [x_ref[part, pl.ds(16 * l, 16), :].astype(F32) for l in range(4)]
        rest = dot(spread_tail, x_ref[part, pl.ds(64, 16), :].reshape(256, 128))
        for f in range(2):
            for l in range(4):
                cut = pl.ds(128 * l, 128)
                add = head[l][:, 8 * f : 8 * f + 8].reshape(128, 128)
                old = latent_ref[f, r, pl.ds(0, 128), cut].astype(F32)
                out[r, f, pl.ds(0, 128), cut] = (old + add).astype(BF)
                at = 64 * l + 32 * f
                old = latent_ref[f, r, pl.ds(128, 32), cut].astype(F32)
                out[r, f, pl.ds(128, 32), cut] = (old + rest[at : at + 32]).astype(BF)
        copies.append(pltpu.make_async_copy(out.at[r], out_any.at[:, r], sems.at[r]))
        copies[r].start()
    for copy in copies:
        copy.wait()


def finish(returned, latents):
    return pl.pallas_call(
        finish_kernel,
        out_shape=jax.ShapeDtypeStruct(latents.shape, BF),
        in_specs=[VMEM, VMEM],
        out_specs=ANY,
        scratch_shapes=[pltpu.VMEM((4, 2, COLS, CH), BF), pltpu.SemaphoreType.DMA((4,))],
        compiler_params=PARAMS,
        name="finish",
    )(returned, latents)


def swap(x, lower):
    return lax.ppermute(x, "slab", [p for i in lower for p in ((i, i + 1), (i + 1, i))])


def on_device(latents, clip_starts, w_space, w_time, w_qkv, w_out):
    count = lax.axis_size("slab")
    even = lax.axis_index("slab") % 2 == 0
    top, bottom = latents[:, :1], latents[:, 3:]
    first = swap(jnp.where(even, bottom, top), range(0, count - 1, 2))
    second = swap(jnp.where(even, top, bottom), range(1, count - 1, 2))
    payload = conv(latents, first, second, w_space)
    arrived = lax.all_to_all(payload, FRAME, split_axis=0, concat_axis=0, tiled=True)
    result = middle(arrived, clip_starts, w_time, w_qkv, w_out)
    returned = lax.all_to_all(result, FRAME, split_axis=0, concat_axis=0, tiled=True)
    return finish(returned, latents)


def solution(mesh):
    finer = Mesh(
        mesh.devices.reshape(8, 4, 2, mesh.shape["slab"]), ("frame_0", "frame_1", "frame_2", "slab")
    )
    return jax.shard_map(
        on_device,
        mesh=finer,
        in_specs=(P(FRAME, "slab", None, None), P(), P(), P(), P(), P()),
        out_specs=P(FRAME, "slab", None, None),
        check_vma=False,
    )
```

```python
import functools

import jax
import jax.numpy as jnp
from jax import lax
from jax.experimental import pallas as pl
from jax.experimental.pallas import tpu as pltpu
from jax.sharding import Mesh
from jax.sharding import PartitionSpec as P

HEADS = 8
FRAME = ("frame_0", "frame_1", "frame_2")
BF = jnp.bfloat16
F32 = jnp.float32
COLS = 160
CH = 512
PAIR = 2 * COLS
TOTAL = 128
VMEM = pl.BlockSpec(memory_space=pltpu.VMEM)
ANY = pl.BlockSpec(memory_space=pl.ANY)
HBM = pl.BlockSpec(memory_space=pltpu.HBM)


def far(x):
    return pltpu.with_memory_space_constraint(x, pltpu.HBM)
PARAMS = pltpu.CompilerParams(vmem_limit_bytes=20 * 1024 * 1024)


def dot(a, b):
    return jnp.dot(a, b, preferred_element_type=F32)


def dot_t(a, b):
    return lax.dot_general(a, b, (((1,), (1,)), ((), ())), preferred_element_type=F32)


def iotas(rows, cols):
    i = lax.broadcasted_iota(jnp.int32, (rows, cols), 0)
    j = lax.broadcasted_iota(jnp.int32, (rows, cols), 1)
    return i, j


def one_hot(hit):
    return jnp.where(hit, 1.0, 0.0).astype(BF)


def tail_source(i):
    return ((i >> 2) & 3) * 64 + (i & 1) * 32 + 2 * (i >> 4) + ((i >> 1) & 1)


def lanes(x, l):
    return x[:, l * 128 : (l + 1) * 128]


def stack_lanes(x):
    return jnp.concatenate([lanes(x, l) for l in range(4)], axis=0)


def tail_matrix():
    i, j = iotas(256, 256)
    return one_hot(tail_source(i) == j)


def pack_row(y, tail, store):
    halves = [y[f * COLS : f * COLS + 128].reshape(16, 8, CH) for f in range(2)]
    head = jnp.concatenate(halves, axis=1).astype(BF)
    for l in range(4):
        store(16 * l, head[:, :, l * 128 : (l + 1) * 128])
    rest = jnp.concatenate([y[f * COLS + 128 : (f + 1) * COLS] for f in range(2)], axis=0)
    store(64, dot(tail, stack_lanes(rest.astype(BF))).astype(BF).reshape(16, 16, 128))


def silu(v):
    return v / (1.0 + jnp.exp(-v))


def spread(x, store):
    wide = x.astype(F32)
    i, _ = iotas(COLS, CH)
    before = jnp.where(i == 0, 0.0, pltpu.roll(wide, 1, 0))
    after = jnp.where(i == COLS - 1, 0.0, pltpu.roll(wide, COLS - 1, 0))
    store(0, x)
    store(1, before.astype(BF))
    store(2, after.astype(BF))


def spread_into(ref, first, x):
    def store(b, v):
        ref[pl.ds(first, COLS), pl.ds(b * CH, CH)] = v

    spread(x, store)


def conv_inner_kernel(
    x_ref, w_any, out_ref, edge_ref, outer_ref, xs, pay, pay_sum, mid_tap, sem, sems
):
    taps = (outer_ref.at[0], mid_tap, outer_ref.at[1])
    order = [(a, b) for a in (1, 2, 0) for b in (1, 0, 2)]
    spot = (1, 0, 2)
    weights = fetch(
        [w_any.at[a, pl.ds(b * CH, CH)] for a, b in order],
        [taps[a].at[pl.ds(spot[b] * CH, CH)] for a, b in order],
        sems,
    )
    for r in range(0, 4):
        for f in range(2):
            spread_into(xs, r * PAIR + f * COLS, x_ref[f, r])
    weights[0].wait()
    centre = []
    for r in range(4):
        x = jnp.concatenate([x_ref[0, r], x_ref[1, r]], axis=0)
        centre.append(dot(x, mid_tap[pl.ds(0, CH), :]))
    edge_ref[0] = centre[0]
    edge_ref[1] = centre[3]
    for n in range(2):
        pay_sum[n] = centre[1 + n]
    tail = tail_matrix()

    def tap(r, a):
        return dot(xs[pl.ds((r + a - 1) * PAIR, PAIR), :], taps[a][...])

    def sides(r):
        return dot(xs[pl.ds(r * PAIR, PAIR), pl.ds(CH, 2 * CH)], mid_tap[pl.ds(CH, 2 * CH), :])

    for copy in weights[1:6]:
        copy.wait()
    edge_ref[0] = edge_ref[0] + sides(0) + tap(0, 2)
    for copy in weights[6:]:
        copy.wait()
    for r in (1, 2):
        y = silu(pay_sum[r - 1] + sides(r) + tap(r, 0) + tap(r, 2))

        def store(first, tiles, r=r):
            pay[pl.ds((r - 1) * 16, 16), pl.ds(first, 16), :] = tiles

        pack_row(y, tail, store)
    copy = pltpu.make_async_copy(pay, out_ref.at[pl.ds(16, 32)], sem)
    copy.start()
    edge_ref[1] = edge_ref[1] + sides(3) + tap(3, 0)
    copy.wait()


def conv_edge_kernel(first_ref, second_ref, edge_ref, w_ref, held_ref, out_ref, xs, pay, sem):
    del held_ref
    even = lax.axis_index("slab") % 2 == 0
    low = jnp.where(even, PAIR, 0)
    for f in range(2):
        spread_into(xs, pl.multiple_of(low + f * COLS, 32), first_ref[f, 0])
        spread_into(xs, pl.multiple_of(PAIR - low + f * COLS, 32), second_ref[f, 0])
    tail = tail_matrix()
    copies = []
    for n in range(2):
        y = silu(edge_ref[n] + dot(xs[pl.ds(n * PAIR, PAIR), :], w_ref[n]))

        def store(first, tiles, n=n):
            pay[n, :, pl.ds(first, 16), :] = tiles

        pack_row(y, tail, store)
        copies.append(
            pltpu.make_async_copy(pay.at[n], out_ref.at[pl.ds(48 * n, 16)], sem.at[n])
        )
        copies[n].start()
    for copy in copies:
        copy.wait()


def conv(latents, first, second, w_space):
    taps = far(w_space.reshape(3, 3 * CH, CH))
    payload = jax.ShapeDtypeStruct((64, 80, 128), BF)
    started, edge, outer = pl.pallas_call(
        conv_inner_kernel,
        out_shape=(
            payload,
            jax.ShapeDtypeStruct((2, PAIR, CH), F32),
            jax.ShapeDtypeStruct((2, 3 * CH, CH), BF),
        ),
        in_specs=[VMEM, HBM],
        out_specs=(ANY, VMEM, VMEM),
        scratch_shapes=[
            pltpu.VMEM((4 * PAIR, 3 * CH), BF),
            pltpu.VMEM((32, 80, 128), BF),
            pltpu.VMEM((2, PAIR, CH), F32),
            pltpu.VMEM((3 * CH, CH), BF),
            pltpu.SemaphoreType.DMA,
            pltpu.SemaphoreType.DMA((9,)),
        ],
        compiler_params=PARAMS,
        cost_estimate=pl.CostEstimate(
            flops=2 * 10 * PAIR * 3 * CH * CH, bytes_accessed=10 << 20, transcendentals=0
        ),
        name="conv_inner",
    )(latents, taps)
    return pl.pallas_call(
        conv_edge_kernel,
        out_shape=payload,
        in_specs=[VMEM, VMEM, VMEM, VMEM, ANY],
        out_specs=ANY,
        scratch_shapes=[
            pltpu.VMEM((2 * PAIR, 3 * CH), BF),
            pltpu.VMEM((2, 16, 80, 128), BF),
            pltpu.SemaphoreType.DMA((2,)),
        ],
        input_output_aliases={4: 0},
        compiler_params=PARAMS,
        name="conv_edge",
    )(first, second, edge, outer, started)


def gather_a(i):
    return ((i >> 1) & 7) * 16 + (i & 1) * 8 + (i >> 4)


def gather_b(i):
    return ((i >> 1) & 7) * 16 + (i >> 5) * 4 + ((i >> 4) & 1) * 2 + (i & 1)


def fetch(sources, buffers, sems):
    copies = [
        pltpu.make_async_copy(source, buffer, sems.at[n])
        for n, (source, buffer) in enumerate(zip(sources, buffers))
    ]
    for copy in copies:
        copy.start()
    return copies


def middle_kernel(
    x_ref, shift_ref, bias_ref, wt_any, wq_any, wo_any, out_ref,
    xs, mixed, qkv, att, res, wt_ref, wq_ref, wo_ref, sems,
):
    weights = fetch((wt_any, wq_any, wo_any), (wt_ref, wq_ref, wo_ref), sems)
    i, j = iotas(128, 128)
    take_a, take_b = one_hot(gather_a(i) == j), one_hot(gather_b(i) == j)
    give_a, give_b = one_hot(gather_a(j) == i), one_hot(gather_b(j) == i)
    for n in range(8):
        part = jnp.concatenate(
            [x_ref[pl.ds(8 * n, 8), pl.ds(16 * l, 16), :].reshape(128, 128) for l in range(4)],
            axis=1,
        )
        rows = dot(take_a, part).astype(BF)
        for k in range(8):
            xs[pl.ds(k * TOTAL + 16 * n, 16), pl.ds(0, CH)] = rows[16 * k : 16 * k + 16]
        rows = dot(take_b, x_ref[pl.ds(8 * n, 8), pl.ds(64, 16), :].reshape(128, 128)).astype(BF)
        for l in range(4):
            for k in range(2):
                at = (2 * l + k) * 16
                xs[pl.ds((8 + k) * TOTAL + 16 * n, 16), pl.ds(128 * l, 128)] = rows[at : at + 16]
    shift = shift_ref[...]
    for k in range(10):
        moved = dot(shift, xs[pl.ds(k * TOTAL, TOTAL), pl.ds(0, CH)]).astype(BF)
        xs[pl.ds(k * TOTAL, TOTAL), pl.ds(CH, CH)] = moved[:TOTAL]
        xs[pl.ds(k * TOTAL, TOTAL), pl.ds(2 * CH, CH)] = moved[TOTAL:]
    weights[0].wait()
    for c in range(2):
        part = pl.ds(640 * c, 640)
        mixed[part, :] = dot(xs[part, :], wt_ref[...]).astype(BF)
    weights[1].wait()
    for c in range(2):
        part = pl.ds(640 * c, 640)
        for t in range(3):
            cut = pl.ds(t * CH, CH)
            qkv[part, cut] = dot(mixed[part, :], wq_ref[:, cut]).astype(BF)

    bias = bias_ref[...]
    _, lane = iotas(TOTAL, 128)
    left = jnp.where(lane < 64, 1.0, 0.0).astype(BF)
    right = jnp.where(lane < 64, 0.0, 1.0).astype(BF)
    scale = BF(0.125)
    weigh = jnp.concatenate([left, right], axis=0)

    def pixel(k, carry):
        rows = pl.ds(pl.multiple_of(k * TOTAL, TOTAL), TOTAL)
        for h in range(4):
            q = qkv[rows, pl.ds(128 * h, 128)]
            key = qkv[rows, pl.ds(CH + 128 * h, 128)]
            v = qkv[rows, pl.ds(2 * CH + 128 * h, 128)]
            keys = jnp.concatenate([key * (left * scale), key * (right * scale)], axis=0)
            s = dot_t(q, keys)
            p = []
            for t in range(2):
                part = lanes(s, t) + bias
                p.append(jnp.exp(part - jnp.max(part, axis=-1, keepdims=True)).astype(BF))
            values = jnp.concatenate([jnp.concatenate([v * left, v * right], axis=0), weigh], axis=1)
            o = dot(jnp.concatenate(p, axis=1), values)
            att[rows, pl.ds(128 * h, 128)] = (o[:, :128] / o[:, 128:]).astype(BF)
        return carry

    lax.fori_loop(0, 10, pixel, 0, unroll=10)
    weights[2].wait()
    for c in range(2):
        part = pl.ds(640 * c, 640)
        res[part, :] = dot(att[part, :], wo_ref[...]).astype(BF)
    for n in range(8):
        rows = jnp.concatenate(
            [res[pl.ds(k * TOTAL + 16 * n, 16), :] for k in range(8)], axis=0
        )
        part = dot(give_a, rows).astype(BF)
        for l in range(4):
            out_ref[pl.ds(8 * n, 8), pl.ds(16 * l, 16), :] = lanes(part, l).reshape(8, 16, 128)
        rows = jnp.concatenate(
            [
                res[pl.ds((8 + k) * TOTAL + 16 * n, 16), pl.ds(128 * l, 128)]
                for l in range(4)
                for k in range(2)
            ],
            axis=0,
        )
        out_ref[pl.ds(8 * n, 8), pl.ds(64, 16), :] = dot(give_b, rows).astype(BF).reshape(8, 16, 128)


def middle(arrived, clip_starts, w_time, w_qkv, w_out):
    clip_ids = jnp.cumsum(clip_starts)
    same = clip_ids[None, :] == clip_ids[:, None]
    i, j = iotas(TOTAL, TOTAL)
    bias = jnp.where(same & (j <= i), 0.0, -1e30).astype(F32)
    shift = jnp.concatenate([one_hot(same & (j == i - 1)), one_hot(same & (j == i - 2))], axis=0)
    return pl.pallas_call(
        middle_kernel,
        out_shape=jax.ShapeDtypeStruct((64, 80, 128), BF),
        in_specs=[VMEM] * 3 + [HBM] * 3,
        out_specs=VMEM,
        scratch_shapes=[
            pltpu.VMEM((1280, 3 * CH), BF),
            pltpu.VMEM((1280, CH), BF),
            pltpu.VMEM((1280, 3 * CH), BF),
            pltpu.VMEM((1280, CH), BF),
            pltpu.VMEM((1280, CH), BF),
            pltpu.VMEM((3 * CH, CH), BF),
            pltpu.VMEM((CH, 3 * CH), BF),
            pltpu.VMEM((CH, CH), BF),
            pltpu.SemaphoreType.DMA((3,)),
        ],
        compiler_params=pltpu.CompilerParams(
            vmem_limit_bytes=20 * 1024 * 1024
        ),
        name="middle",
    )(arrived, shift, bias, far(w_time.reshape(3 * CH, CH)), far(w_qkv), far(w_out))


def finish_kernel(x_ref, latent_ref, out_any, out, sems):
    i, j = iotas(256, 256)
    spread_tail = one_hot(tail_source(j) == i)
    copies = []
    for r in range(4):
        part = pl.ds(16 * r, 16)
        head = [x_ref[part, pl.ds(16 * l, 16), :].astype(F32) for l in range(4)]
        rest = dot(spread_tail, x_ref[part, pl.ds(64, 16), :].reshape(256, 128))
        for f in range(2):
            for l in range(4):
                cut = pl.ds(128 * l, 128)
                add = head[l][:, 8 * f : 8 * f + 8].reshape(128, 128)
                old = latent_ref[f, r, pl.ds(0, 128), cut].astype(F32)
                out[r, f, pl.ds(0, 128), cut] = (old + add).astype(BF)
                at = 64 * l + 32 * f
                old = latent_ref[f, r, pl.ds(128, 32), cut].astype(F32)
                out[r, f, pl.ds(128, 32), cut] = (old + rest[at : at + 32]).astype(BF)
        copies.append(pltpu.make_async_copy(out.at[r], out_any.at[:, r], sems.at[r]))
        copies[r].start()
    for copy in copies:
        copy.wait()


def finish(returned, latents):
    return pl.pallas_call(
        finish_kernel,
        out_shape=jax.ShapeDtypeStruct(latents.shape, BF),
        in_specs=[VMEM, VMEM],
        out_specs=ANY,
        scratch_shapes=[pltpu.VMEM((4, 2, COLS, CH), BF), pltpu.SemaphoreType.DMA((4,))],
        compiler_params=PARAMS,
        name="finish",
    )(returned, latents)


def swap(x, lower):
    return lax.ppermute(x, "slab", [p for i in lower for p in ((i, i + 1), (i + 1, i))])


def on_device(latents, clip_starts, w_space, w_time, w_qkv, w_out):
    count = lax.axis_size("slab")
    even = lax.axis_index("slab") % 2 == 0
    top, bottom = latents[:, :1], latents[:, 3:]
    first = swap(jnp.where(even, bottom, top), range(0, count - 1, 2))
    second = swap(jnp.where(even, top, bottom), range(1, count - 1, 2))
    payload = conv(latents, first, second, w_space)
    arrived = lax.all_to_all(payload, FRAME, split_axis=0, concat_axis=0, tiled=True)
    result = middle(arrived, clip_starts, w_time, w_qkv, w_out)
    returned = lax.all_to_all(result, FRAME, split_axis=0, concat_axis=0, tiled=True)
    return finish(returned, latents)


def solution(mesh):
    finer = Mesh(
        mesh.devices.reshape(8, 4, 2, mesh.shape["slab"]), ("frame_0", "frame_1", "frame_2", "slab")
    )
    return jax.shard_map(
        on_device,
        mesh=finer,
        in_specs=(P(FRAME, "slab", None, None), P(), P(), P(), P(), P()),
        out_specs=P(FRAME, "slab", None, None),
        check_vma=False,
    )
```

```python
import functools

import jax
import jax.numpy as jnp
from jax import lax
from jax.experimental import pallas as pl
from jax.experimental.pallas import tpu as pltpu
from jax.sharding import Mesh
from jax.sharding import PartitionSpec as P

HEADS = 8
FRAME = ("frame_0", "frame_1", "frame_2")
BF = jnp.bfloat16
F32 = jnp.float32
COLS = 160
CH = 512
PAIR = 2 * COLS
TOTAL = 128
VMEM = pl.BlockSpec(memory_space=pltpu.VMEM)
ANY = pl.BlockSpec(memory_space=pl.ANY)
HBM = pl.BlockSpec(memory_space=pltpu.HBM)


def far(x):
    return pltpu.with_memory_space_constraint(x, pltpu.HBM)
PARAMS = pltpu.CompilerParams(vmem_limit_bytes=20 * 1024 * 1024)


def dot(a, b):
    return jnp.dot(a, b, preferred_element_type=F32)


def dot_t(a, b):
    return lax.dot_general(a, b, (((1,), (1,)), ((), ())), preferred_element_type=F32)


def iotas(rows, cols):
    i = lax.broadcasted_iota(jnp.int32, (rows, cols), 0)
    j = lax.broadcasted_iota(jnp.int32, (rows, cols), 1)
    return i, j


def one_hot(hit):
    return jnp.where(hit, 1.0, 0.0).astype(BF)


def tail_source(i):
    return ((i >> 2) & 3) * 64 + (i & 1) * 32 + 2 * (i >> 4) + ((i >> 1) & 1)


def lanes(x, l):
    return x[:, l * 128 : (l + 1) * 128]


def stack_lanes(x):
    return jnp.concatenate([lanes(x, l) for l in range(4)], axis=0)


def tail_matrix():
    i, j = iotas(256, 256)
    return one_hot(tail_source(i) == j)


def pack_row(y, tail, store):
    halves = [y[f * COLS : f * COLS + 128].reshape(16, 8, CH) for f in range(2)]
    head = jnp.concatenate(halves, axis=1).astype(BF)
    for l in range(4):
        store(16 * l, head[:, :, l * 128 : (l + 1) * 128])
    rest = jnp.concatenate([y[f * COLS + 128 : (f + 1) * COLS] for f in range(2)], axis=0)
    store(64, dot(tail, stack_lanes(rest.astype(BF))).astype(BF).reshape(16, 16, 128))


def silu(v):
    return v / (1.0 + jnp.exp(-v))


def spread(x, store):
    wide = x.astype(F32)
    i, _ = iotas(COLS, CH)
    before = jnp.where(i == 0, 0.0, pltpu.roll(wide, 1, 0))
    after = jnp.where(i == COLS - 1, 0.0, pltpu.roll(wide, COLS - 1, 0))
    store(0, x)
    store(1, before.astype(BF))
    store(2, after.astype(BF))


def spread_into(ref, first, x):
    def store(b, v):
        ref[pl.ds(first, COLS), pl.ds(b * CH, CH)] = v

    spread(x, store)


def conv_inner_kernel(
    x_ref, w_any, out_ref, edge_ref, outer_ref, xs, pay, pay_sum, mid_tap, sem, sems
):
    taps = (outer_ref.at[0], mid_tap, outer_ref.at[1])
    order = [(a, b) for a in (1, 2, 0) for b in (1, 0, 2)]
    spot = (1, 0, 2)
    weights = fetch(
        [w_any.at[a, pl.ds(b * CH, CH)] for a, b in order],
        [taps[a].at[pl.ds(spot[b] * CH, CH)] for a, b in order],
        sems,
    )
    for r in range(0, 2):
        for f in range(2):
            spread_into(xs, r * PAIR + f * COLS, x_ref[f, r])
    weights[0].wait()
    centre = []
    for r in range(4):
        x = jnp.concatenate([x_ref[0, r], x_ref[1, r]], axis=0)
        centre.append(dot(x, mid_tap[pl.ds(0, CH), :]))
    edge_ref[0] = centre[0]
    edge_ref[1] = centre[3]
    for n in range(2):
        pay_sum[n] = centre[1 + n]
    for r in range(2, 4):
        for f in range(2):
            spread_into(xs, r * PAIR + f * COLS, x_ref[f, r])
    tail = tail_matrix()

    def tap(r, a):
        return dot(xs[pl.ds((r + a - 1) * PAIR, PAIR), :], taps[a][...])

    def sides(r):
        return dot(xs[pl.ds(r * PAIR, PAIR), pl.ds(CH, 2 * CH)], mid_tap[pl.ds(CH, 2 * CH), :])

    for copy in weights[1:6]:
        copy.wait()
    edge_ref[0] = edge_ref[0] + sides(0) + tap(0, 2)
    for copy in weights[6:]:
        copy.wait()
    for r in (1, 2):
        y = silu(pay_sum[r - 1] + sides(r) + tap(r, 0) + tap(r, 2))

        def store(first, tiles, r=r):
            pay[pl.ds((r - 1) * 16, 16), pl.ds(first, 16), :] = tiles

        pack_row(y, tail, store)
    copy = pltpu.make_async_copy(pay, out_ref.at[pl.ds(16, 32)], sem)
    copy.start()
    edge_ref[1] = edge_ref[1] + sides(3) + tap(3, 0)
    copy.wait()


def conv_edge_kernel(first_ref, second_ref, edge_ref, w_ref, held_ref, out_ref, xs, pay, sem):
    del held_ref
    even = lax.axis_index("slab") % 2 == 0
    for f in range(2):
        first, second = first_ref[f, 0].astype(F32), second_ref[f, 0].astype(F32)
        spread_into(xs, f * COLS, jnp.where(even, second, first).astype(BF))
        spread_into(xs, PAIR + f * COLS, jnp.where(even, first, second).astype(BF))
    tail = tail_matrix()
    copies = []
    for n in range(2):
        y = silu(edge_ref[n] + dot(xs[pl.ds(n * PAIR, PAIR), :], w_ref[n]))

        def store(first, tiles, n=n):
            pay[n, :, pl.ds(first, 16), :] = tiles

        pack_row(y, tail, store)
        copies.append(
            pltpu.make_async_copy(pay.at[n], out_ref.at[pl.ds(48 * n, 16)], sem.at[n])
        )
        copies[n].start()
    for copy in copies:
        copy.wait()


def conv(latents, first, second, w_space):
    taps = far(w_space.reshape(3, 3 * CH, CH))
    payload = jax.ShapeDtypeStruct((64, 80, 128), BF)
    started, edge, outer = pl.pallas_call(
        conv_inner_kernel,
        out_shape=(
            payload,
            jax.ShapeDtypeStruct((2, PAIR, CH), F32),
            jax.ShapeDtypeStruct((2, 3 * CH, CH), BF),
        ),
        in_specs=[VMEM, HBM],
        out_specs=(ANY, VMEM, VMEM),
        scratch_shapes=[
            pltpu.VMEM((4 * PAIR, 3 * CH), BF),
            pltpu.VMEM((32, 80, 128), BF),
            pltpu.VMEM((2, PAIR, CH), F32),
            pltpu.VMEM((3 * CH, CH), BF),
            pltpu.SemaphoreType.DMA,
            pltpu.SemaphoreType.DMA((9,)),
        ],
        compiler_params=PARAMS,
        cost_estimate=pl.CostEstimate(
            flops=2 * 10 * PAIR * 3 * CH * CH, bytes_accessed=10 << 20, transcendentals=0
        ),
        name="conv_inner",
    )(latents, taps)
    return pl.pallas_call(
        conv_edge_kernel,
        out_shape=payload,
        in_specs=[VMEM, VMEM, VMEM, VMEM, ANY],
        out_specs=ANY,
        scratch_shapes=[
            pltpu.VMEM((2 * PAIR, 3 * CH), BF),
            pltpu.VMEM((2, 16, 80, 128), BF),
            pltpu.SemaphoreType.DMA((2,)),
        ],
        input_output_aliases={4: 0},
        compiler_params=PARAMS,
        name="conv_edge",
    )(first, second, edge, outer, started)


def gather_a(i):
    return ((i >> 1) & 7) * 16 + (i & 1) * 8 + (i >> 4)


def gather_b(i):
    return ((i >> 1) & 7) * 16 + (i >> 5) * 4 + ((i >> 4) & 1) * 2 + (i & 1)


def fetch(sources, buffers, sems):
    copies = [
        pltpu.make_async_copy(source, buffer, sems.at[n])
        for n, (source, buffer) in enumerate(zip(sources, buffers))
    ]
    for copy in copies:
        copy.start()
    return copies


def middle_kernel(
    x_ref, shift_ref, bias_ref, wt_any, wq_any, wo_any, out_ref,
    xs, mixed, qkv, att, res, wt_ref, wq_ref, wo_ref, sems,
):
    weights = fetch((wt_any, wq_any, wo_any), (wt_ref, wq_ref, wo_ref), sems)
    i, j = iotas(128, 128)
    take_a, take_b = one_hot(gather_a(i) == j), one_hot(gather_b(i) == j)
    give_a, give_b = one_hot(gather_a(j) == i), one_hot(gather_b(j) == i)
    for n in range(8):
        part = jnp.concatenate(
            [x_ref[pl.ds(8 * n, 8), pl.ds(16 * l, 16), :].reshape(128, 128) for l in range(4)],
            axis=1,
        )
        rows = dot(take_a, part).astype(BF)
        for k in range(8):
            xs[pl.ds(k * TOTAL + 16 * n, 16), pl.ds(0, CH)] = rows[16 * k : 16 * k + 16]
        rows = dot(take_b, x_ref[pl.ds(8 * n, 8), pl.ds(64, 16), :].reshape(128, 128)).astype(BF)
        for l in range(4):
            for k in range(2):
                at = (2 * l + k) * 16
                xs[pl.ds((8 + k) * TOTAL + 16 * n, 16), pl.ds(128 * l, 128)] = rows[at : at + 16]
    shift = shift_ref[...]
    for k in range(10):
        moved = dot(shift, xs[pl.ds(k * TOTAL, TOTAL), pl.ds(0, CH)]).astype(BF)
        xs[pl.ds(k * TOTAL, TOTAL), pl.ds(CH, CH)] = moved[:TOTAL]
        xs[pl.ds(k * TOTAL, TOTAL), pl.ds(2 * CH, CH)] = moved[TOTAL:]
    weights[0].wait()
    for c in range(2):
        part = pl.ds(640 * c, 640)
        mixed[part, :] = dot(xs[part, :], wt_ref[...]).astype(BF)
    weights[1].wait()
    for c in range(2):
        part = pl.ds(640 * c, 640)
        for t in range(3):
            cut = pl.ds(t * CH, CH)
            qkv[part, cut] = dot(mixed[part, :], wq_ref[:, cut]).astype(BF)

    bias = bias_ref[...]
    _, lane = iotas(TOTAL, 128)
    left = jnp.where(lane < 64, 1.0, 0.0).astype(BF)
    right = jnp.where(lane < 64, 0.0, 1.0).astype(BF)
    scale = BF(0.125)
    weigh = jnp.concatenate([left, right], axis=0)

    def pixel(k, carry):
        rows = pl.ds(pl.multiple_of(k * TOTAL, TOTAL), TOTAL)
        for h in range(4):
            q = qkv[rows, pl.ds(128 * h, 128)]
            key = qkv[rows, pl.ds(CH + 128 * h, 128)]
            v = qkv[rows, pl.ds(2 * CH + 128 * h, 128)]
            keys = jnp.concatenate([key * (left * scale), key * (right * scale)], axis=0)
            s = dot_t(q, keys)
            p = []
            for t in range(2):
                part = lanes(s, t) + bias
                p.append(jnp.exp(part - jnp.max(part, axis=-1, keepdims=True)).astype(BF))
            values = jnp.concatenate([jnp.concatenate([v * left, v * right], axis=0), weigh], axis=1)
            o = dot(jnp.concatenate(p, axis=1), values)
            att[rows, pl.ds(128 * h, 128)] = (o[:, :128] / o[:, 128:]).astype(BF)
        return carry

    lax.fori_loop(0, 10, pixel, 0, unroll=10)
    weights[2].wait()
    for c in range(2):
        part = pl.ds(640 * c, 640)
        res[part, :] = dot(att[part, :], wo_ref[...]).astype(BF)
    for n in range(8):
        rows = jnp.concatenate(
            [res[pl.ds(k * TOTAL + 16 * n, 16), :] for k in range(8)], axis=0
        )
        part = dot(give_a, rows).astype(BF)
        for l in range(4):
            out_ref[pl.ds(8 * n, 8), pl.ds(16 * l, 16), :] = lanes(part, l).reshape(8, 16, 128)
        rows = jnp.concatenate(
            [
                res[pl.ds((8 + k) * TOTAL + 16 * n, 16), pl.ds(128 * l, 128)]
                for l in range(4)
                for k in range(2)
            ],
            axis=0,
        )
        out_ref[pl.ds(8 * n, 8), pl.ds(64, 16), :] = dot(give_b, rows).astype(BF).reshape(8, 16, 128)


def middle(arrived, clip_starts, w_time, w_qkv, w_out):
    clip_ids = jnp.cumsum(clip_starts)
    same = clip_ids[None, :] == clip_ids[:, None]
    i, j = iotas(TOTAL, TOTAL)
    bias = jnp.where(same & (j <= i), 0.0, -1e30).astype(F32)
    shift = jnp.concatenate([one_hot(same & (j == i - 1)), one_hot(same & (j == i - 2))], axis=0)
    return pl.pallas_call(
        middle_kernel,
        out_shape=jax.ShapeDtypeStruct((64, 80, 128), BF),
        in_specs=[VMEM] * 3 + [HBM] * 3,
        out_specs=VMEM,
        scratch_shapes=[
            pltpu.VMEM((1280, 3 * CH), BF),
            pltpu.VMEM((1280, CH), BF),
            pltpu.VMEM((1280, 3 * CH), BF),
            pltpu.VMEM((1280, CH), BF),
            pltpu.VMEM((1280, CH), BF),
            pltpu.VMEM((3 * CH, CH), BF),
            pltpu.VMEM((CH, 3 * CH), BF),
            pltpu.VMEM((CH, CH), BF),
            pltpu.SemaphoreType.DMA((3,)),
        ],
        compiler_params=pltpu.CompilerParams(
            vmem_limit_bytes=20 * 1024 * 1024
        ),
        name="middle",
    )(arrived, shift, bias, far(w_time.reshape(3 * CH, CH)), far(w_qkv), far(w_out))


def finish_kernel(x_ref, latent_ref, out_any, out, sems):
    i, j = iotas(256, 256)
    spread_tail = one_hot(tail_source(j) == i)
    copies = []
    for r in range(4):
        part = pl.ds(16 * r, 16)
        head = [x_ref[part, pl.ds(16 * l, 16), :].astype(F32) for l in range(4)]
        rest = dot(spread_tail, x_ref[part, pl.ds(64, 16), :].reshape(256, 128))
        for f in range(2):
            for l in range(4):
                cut = pl.ds(128 * l, 128)
                add = head[l][:, 8 * f : 8 * f + 8].reshape(128, 128)
                old = latent_ref[f, r, pl.ds(0, 128), cut].astype(F32)
                out[r, f, pl.ds(0, 128), cut] = (old + add).astype(BF)
                at = 64 * l + 32 * f
                old = latent_ref[f, r, pl.ds(128, 32), cut].astype(F32)
                out[r, f, pl.ds(128, 32), cut] = (old + rest[at : at + 32]).astype(BF)
        copies.append(pltpu.make_async_copy(out.at[r], out_any.at[:, r], sems.at[r]))
        copies[r].start()
    for copy in copies:
        copy.wait()


def finish(returned, latents):
    return pl.pallas_call(
        finish_kernel,
        out_shape=jax.ShapeDtypeStruct(latents.shape, BF),
        in_specs=[VMEM, VMEM],
        out_specs=ANY,
        scratch_shapes=[pltpu.VMEM((4, 2, COLS, CH), BF), pltpu.SemaphoreType.DMA((4,))],
        compiler_params=PARAMS,
        name="finish",
    )(returned, latents)


def swap(x, lower):
    return lax.ppermute(x, "slab", [p for i in lower for p in ((i, i + 1), (i + 1, i))])


def on_device(latents, clip_starts, w_space, w_time, w_qkv, w_out):
    count = lax.axis_size("slab")
    even = lax.axis_index("slab") % 2 == 0
    top, bottom = latents[:, :1], latents[:, 3:]
    first = swap(jnp.where(even, bottom, top), range(0, count - 1, 2))
    second = swap(jnp.where(even, top, bottom), range(1, count - 1, 2))
    payload = conv(latents, first, second, w_space)
    arrived = lax.all_to_all(payload, FRAME, split_axis=0, concat_axis=0, tiled=True)
    result = middle(arrived, clip_starts, w_time, w_qkv, w_out)
    returned = lax.all_to_all(result, FRAME, split_axis=0, concat_axis=0, tiled=True)
    return finish(returned, latents)


def solution(mesh):
    finer = Mesh(
        mesh.devices.reshape(8, 4, 2, mesh.shape["slab"]), ("frame_0", "frame_1", "frame_2", "slab")
    )
    return jax.shard_map(
        on_device,
        mesh=finer,
        in_specs=(P(FRAME, "slab", None, None), P(), P(), P(), P(), P()),
        out_specs=P(FRAME, "slab", None, None),
        check_vma=False,
    )
```
